256 devices in a mesh: seq: 32 (over y, z_lo, core), head: 8 (over x, z_hi).
Axes of the slice: x: 4, y: 4, z: 8 (z_hi: 2, z_lo: 4; z = z_hi * 4 + z_lo), core: 2. Of those that a mesh axis runs over, the one named last changes fastest.
Arguments:
- queries: bfloat16 [4096, 8192], P('seq', 'head'), may hold values from -48 to 48
- keyval: bfloat16 [4096, 2048], P('seq', 'head'), may hold values from -48 to 48
- grad_out: bfloat16 [4096, 8192], P('seq', 'head'), may hold values from -6 to 6
- doc_ids: int32 [4096], P('seq'), may hold values from 0 to 3, never falling along the last dimension, each value on 1 to 2048 neighbouring positions
- deltas: bfloat16 [8, 4096, 8192], P('head', 'seq'), may hold values from -6 to 6
- node_weights: bfloat16 [8192, 2048], P('head', 'seq'), may hold values from -0.0625 to 0.0625
- layer_slot: int32 [8], replicated, may hold values from 0 to 7, each once
Outputs:
- grad_query: bfloat16 [4096, 8192], P('seq', 'head')
- grad_keyval: bfloat16 [4096, 2048], P('seq', 'head')
- scores: float32 [8, 16], replicated
The draws below stay inside these ranges and needn't reach their ends.
Inputs may be any that keep to these rules, and one draw needn't show every extreme that they name: `layer_slot`: each of the 8 layers stands in exactly one slot. `doc_ids`: never falling along the sequence.
All inputs are finite; a program needn't handle non-finite values.
Results may differ from the reference program's by a relative error of at most 0.013.
Values may be sent and summed in bfloat16 or wider, within the bound.
A program may use at most 64 MiB of HBM per device.

```python
import math
import jax
import jax.numpy as jnp
import numpy as np
from jax import lax

D = 8192
H = 64
KVH = 8
HD = 128
SEQ = 4096
LAYERS = 8


def attention_pair(key):
    base = jax.random.fold_in(key, 7)
    key_query, key_keys = jax.random.split(base, 2)
    queries = jnp.clip(jax.random.normal(key_query, (SEQ, H * HD), jnp.float32), -4.0, 4.0)
    keyval = jnp.clip(jax.random.normal(key_keys, (SEQ, KVH * 2 * HD), jnp.float32), -4.0, 4.0)
    return (queries, keyval)


def draw_queries(key, part):
    return attention_pair(key)[0].astype(jnp.bfloat16)


def draw_keyval(key, part):
    return attention_pair(key)[1].astype(jnp.bfloat16)


def levels(key, dims, cuts, smallest, largest):
    def one(dim, shards_of):
        steps = jax.random.uniform(jax.random.fold_in(jax.random.fold_in(key, 6), dim), (shards_of,), jnp.float32, smallest / len(cuts), largest / len(cuts))
        return jnp.repeat(jnp.exp(steps), dims[dim] // shards_of).reshape((-1,) + (1,) * (len(dims) - dim - 1))

    loudness = one(*cuts[0])
    for cut in cuts[1:]:
        loudness = loudness * one(*cut)
    return loudness


def profile(count, total, most, skew):
    weights = [(1 << 20) // math.isqrt(grade ** skew) + 1 for grade in range(2, count + 1)]
    rest, counts = total - most - (count - 1), [1] * (count - 1)
    while rest > 0:
        candidates = [i for i in range(count - 1) if counts[i] < most]
        whole, budget = sum([weights[i] for i in candidates]), rest
        for i in candidates:
            more = min(most - counts[i], max(1, budget * weights[i] // whole), rest)
            counts[i] = counts[i] + more
            rest = rest - more
    return np.array([most] + counts)


def ragged_sizes(own_key, number_of, total, bound, skew):
    if number_of == 2:
        one = jax.random.randint(own_key, (), max(1, total - bound), min(bound, total - 1) + 1)
        return jnp.stack([one, total - one])
    lengths = jnp.asarray(profile(number_of, total, bound, skew), jnp.int32)
    pairs = (number_of - 1) // 2
    donor, receiver = lengths[1:1 + 2 * pairs:2], lengths[2:2 + 2 * pairs:2]
    slack = jnp.minimum(donor - 1, bound - receiver)
    moved = jax.random.randint(jax.random.fold_in(own_key, 1), (pairs,), 0, 1 << 20) % (slack + 1)
    lengths = lengths.at[1:1 + 2 * pairs:2].set(donor - moved).at[2:2 + 2 * pairs:2].set(receiver + moved)
    return lengths[jax.random.permutation(jax.random.fold_in(own_key, 2), number_of)]


def scatter_about(key, dims, width, bound, cuts=(), kind=jnp.bfloat16):
    drawn = jax.random.normal(key, dims, jnp.float32) * width
    if len(cuts) > 0:
        drawn = levels(key, dims, cuts, -0.22, 0.18) * drawn
    return jnp.clip(drawn, min=-bound, max=bound).astype(kind)


def setup_inputs(seed: int = 0) -> dict:
    arg_keys = jax.random.split(jax.random.key(seed), 8)
    return {
        "queries": draw_queries(jax.random.fold_in(arg_keys[7], 71), 0),
        "keyval": draw_keyval(jax.random.fold_in(arg_keys[7], 71), 0),
        "grad_out": scatter_about(arg_keys[2], (SEQ, H * HD), 1.0, 6.0, ((0, 32), (1, 8))),
        "doc_ids": jnp.searchsorted(jnp.cumsum(ragged_sizes(arg_keys[3], 4, SEQ, SEQ // 2, 0)), jnp.arange(SEQ), side="right").astype(jnp.int32),
        "deltas": scatter_about(arg_keys[4], (LAYERS, SEQ, D), 1.0, 6.0, ((0, 8), (1, 32))),
        "node_weights": scatter_about(arg_keys[5], (D, KVH * 2 * HD), D ** -0.5, 0.0625, ((0, 8), (1, 32))),
        "layer_slot": jax.random.permutation(arg_keys[6], LAYERS).astype(jnp.int32),
    }


def reference(queries, keyval, grad_out, doc_ids, deltas, node_weights, layer_slot):
    group_size = H // KVH
    score_scale = 1.0 / math.sqrt(HD)
    positions = jnp.arange(SEQ, dtype=jnp.int32)
    allowed = (doc_ids[None, :] == doc_ids[:, None]) & (positions[None, :] <= positions[:, None])
    query_grid = queries.reshape(SEQ, KVH, group_size, HD)
    out_grid = grad_out.reshape(SEQ, KVH, group_size, HD)
    kv_grid = keyval.reshape(SEQ, KVH, 2, HD)

    def one_group(group_index):
        key_rows = kv_grid[:, group_index, 0]
        value_rows = kv_grid[:, group_index, 1]

        def one_head(head_index):
            query_rows = query_grid[:, group_index, head_index]
            out_rows = out_grid[:, group_index, head_index]
            logits = jnp.dot(query_rows, key_rows.T, preferred_element_type=jnp.float32) * score_scale
            logits = jnp.where(allowed, logits, -jnp.inf)
            row_max = lax.optimization_barrier(jnp.max(logits, axis=1, keepdims=True))
            weights = jnp.exp(logits - row_max)
            probs = weights / lax.optimization_barrier(jnp.sum(weights, axis=1, keepdims=True))
            attn_out = jnp.dot(probs, value_rows.astype(jnp.float32), precision=lax.Precision.HIGHEST)
            row_dot = lax.optimization_barrier(jnp.sum(out_rows.astype(jnp.float32) * attn_out, axis=1, keepdims=True))
            probs_low = probs.astype(jnp.bfloat16)
            grad_probs = jnp.dot(out_rows, value_rows.T, preferred_element_type=jnp.float32)
            grad_logits = (probs * (grad_probs - row_dot)).astype(jnp.bfloat16)
            grad_q = jnp.dot(grad_logits, key_rows, preferred_element_type=jnp.float32) * score_scale
            grad_k = jnp.dot(grad_logits.T, query_rows, preferred_element_type=jnp.float32) * score_scale
            grad_v = jnp.dot(probs_low.T, out_rows, preferred_element_type=jnp.float32)
            return (grad_q.astype(jnp.bfloat16), grad_k, grad_v)
        grad_q, grad_k, grad_v = lax.map(one_head, jnp.arange(group_size))
        return (grad_q, lax.optimization_barrier(jnp.sum(grad_k, axis=0)), lax.optimization_barrier(jnp.sum(grad_v, axis=0)))
    grad_q, grad_k, grad_v = lax.map(one_group, jnp.arange(KVH))
    grad_query = jnp.transpose(grad_q, (2, 0, 1, 3)).reshape(SEQ, H * HD)
    grad_both = jnp.stack((grad_k, grad_v), axis=1)
    grad_keyval = jnp.transpose(grad_both, (2, 0, 1, 3)).reshape(SEQ, KVH * 2 * HD).astype(jnp.bfloat16)
    node_count = 2 * KVH
    grad_nodes = grad_keyval.reshape(SEQ, node_count, HD)
    weight_nodes = node_weights.reshape(D, node_count, HD)

    def one_node(node_index):
        node_grad = jnp.dot(grad_nodes[:, node_index], weight_nodes[:, node_index].T, preferred_element_type=jnp.float32)

        def one_layer(slot_index):
            return jnp.sum(deltas[slot_index].astype(jnp.float32) * node_grad)
        return lax.map(one_layer, jnp.arange(LAYERS))
    slot_scores = lax.map(one_node, jnp.arange(node_count)).T / math.sqrt(SEQ)
    placing = (layer_slot[:, None] == jnp.arange(LAYERS, dtype=jnp.int32)[None, :]).astype(jnp.float32)
    scores = jnp.dot(placing.T, slot_scores, precision=lax.Precision.HIGHEST)
    return (grad_query, grad_keyval, scores)
```

```python
import math

import jax
import jax.numpy as jnp
from jax import lax
from jax.experimental import pallas as pl
from jax.experimental.pallas import tpu as pltpu
from jax.sharding import PartitionSpec as P

HD = 128
GROUP = 8
ROWS = 128
SPAN = 9
NEG = -1e30
FLOOR = -1e29
SCALE = 1.0 / math.sqrt(HD)
EXP_SCALE = SCALE * math.log2(math.e)
MESH = pl.DeviceIdType.MESH
NT = (((1,), (1,)), ((), ()))


def remote(src, dst, send, recv, seq, head):
    return pltpu.make_async_remote_copy(
        src_ref=src,
        dst_ref=dst,
        send_sem=send,
        recv_sem=recv,
        device_id=(seq, head),
        device_id_type=MESH,
    )


def kernel(
    q_ref,
    kv_ref,
    go_ref,
    doc_ref,
    del_ref,
    wt_ref,
    gq_ref,
    gkv_ref,
    sc_ref,
    q8,
    go8,
    kvbuf,
    docbuf,
    docq,
    bias,
    ebuf,
    dpbuf,
    mxb,
    lsb,
    dsb,
    stat,
    strecv,
    pbuf,
    dsbuf,
    sendbuf,
    dkvrecv,
    ownbuf,
    dqbuf,
    dqrecv,
    dbuf,
    wbuf,
    pbig,
    gbuf,
    arsrc,
    ar1,
    ar2,
    ar3,
    kvs,
    kvr,
    docs,
    docr,
    qs,
    qr,
    sts,
    str_,
    dks,
    dkr,
    dqs,
    dqr,
    dls,
    dlr,
    loc,
    ays,
    ayr,
    azps,
    azpr,
    azms,
    azmr,
    bzps,
    bzpr,
    bzms,
    bzmr,
    bys,
    byr,
    fas,
    far,
    fbs,
    fbr,
    g1s,
    g1r,
    gxs,
    gxr,
    a1s,
    a1r,
    a2s,
    a2r,
    a3s,
    a3r,
):
    s = lax.axis_index("seq")
    h = lax.axis_index("head")
    core = lax.rem(s, 2)
    chip = s // 2
    zl = lax.rem(chip, 4)
    y = chip // 4
    zh = lax.rem(h, 2)
    x = h // 2
    z = zh * 4 + zl
    sib = s + 1 - 2 * core

    def at_yz(y_, z_, c_):
        return (y_ * 4 + lax.rem(z_, 4)) * 2 + c_, x * 2 + z_ // 4

    def kv_copy(j):
        return remote(kv_ref, kvbuf.at[j], kvs.at[j], kvr.at[j], lax.rem(s + 2 * j, 32), h)

    def doc_copy(j):
        return remote(doc_ref, docbuf.at[j], docs.at[j], docr.at[j], lax.rem(s + 2 * j, 32), h)

    def q_copy(g):
        return remote(
            q_ref.at[:, pl.ds(g * HD, HD)],
            q8.at[g, pl.ds(core * ROWS, ROWS)],
            qs.at[g],
            qr.at[g],
            sib,
            h,
        )

    def go_copy(g):
        return remote(
            go_ref.at[:, pl.ds(g * HD, HD)],
            go8.at[g, pl.ds(core * ROWS, ROWS)],
            qs.at[8 + g],
            qr.at[8 + g],
            sib,
            h,
        )

    def q_wait(g):
        return remote(
            q_ref.at[:, pl.ds(g * HD, HD)],
            q8.at[g, pl.ds((1 - core) * ROWS, ROWS)],
            qs.at[g],
            qr.at[g],
            sib,
            h,
        )

    def go_wait(g):
        return remote(
            go_ref.at[:, pl.ds(g * HD, HD)],
            go8.at[g, pl.ds((1 - core) * ROWS, ROWS)],
            qs.at[8 + g],
            qr.at[8 + g],
            sib,
            h,
        )

    docq_send = remote(doc_ref, docq.at[core], docs.at[0], docr.at[0], sib, h)
    docq_wait = remote(doc_ref, docq.at[1 - core], docs.at[0], docr.at[0], sib, h)
    docq_send.start()
    for g in range(GROUP):
        q_copy(g).start()
        go_copy(g).start()
    for j in range(1, SPAN):

        @pl.when(chip + j <= 15)
        def _():
            doc_copy(j).start()
            kv_copy(j).start()

    def del_copy(k):
        xt = lax.rem(x + k, 4)
        return remote(
            del_ref.at[:, pl.ds(xt * 2048, 2048)],
            dbuf.at[x],
            dls.at[k],
            dlr.at[k],
            s,
            xt * 2 + zh,
        )

    def del_wait(k):
        xf = lax.rem(x + 4 - k, 4)
        return remote(
            del_ref.at[:, pl.ds(xf * 2048, 2048)],
            dbuf.at[xf],
            dls.at[k],
            dlr.at[k],
            s,
            xf * 2 + zh,
        )

    for k in range(1, 4):
        del_copy(k).start()
    own_delta = pltpu.make_async_copy(
        del_ref.at[:, pl.ds(x * 2048, 2048)], dbuf.at[x], loc.at[0]
    )
    own_delta.start()

    LO, HI = pl.ds(0, 512), pl.ds(512, 512)
    own_w = pltpu.make_async_copy(wt_ref, wbuf.at[zh, y, zl, core], loc.at[1])
    own_w.start()

    def ay_copy(k):
        seq, head = at_yz(lax.rem(y + k, 4), z, core)
        return remote(
            wt_ref.at[:, LO], wbuf.at[zh, y, zl, core, :, LO], ays.at[k], ayr.at[k], seq, head
        )

    def ay_wait(k):
        yf = lax.rem(y + 4 - k, 4)
        return remote(
            wt_ref.at[:, LO], wbuf.at[zh, yf, zl, core, :, LO], ays.at[k], ayr.at[k], s, h
        )

    def z_set(o, colour):
        if colour == 0:
            return wbuf.at[o // 4, :, lax.rem(o, 4), core, :, LO]
        return wbuf.at[o // 4, y, lax.rem(o, 4), core, :, HI]

    def zp_copy(k, colour, wait):
        o = lax.rem(z - k + 8 + (0 if wait else 1), 8)
        ss, rs = (azps, azpr) if colour == 0 else (bzps, bzpr)
        seq, head = at_yz(y, lax.rem(z + 1, 8), core)
        return remote(z_set(o, colour), z_set(o, colour), ss.at[k], rs.at[k], seq, head)

    def zm_copy(k, colour, wait):
        o = lax.rem(z + k - (0 if wait else 1), 8)
        ss, rs = (azms, azmr) if colour == 0 else (bzms, bzmr)
        seq, head = at_yz(y, lax.rem(z + 7, 8), core)
        return remote(z_set(o, colour), z_set(o, colour), ss.at[k], rs.at[k], seq, head)

    def by_set(y_):
        return wbuf.at[:, y_, :, core, :, HI]

    def by_copy(k):
        seq, head = at_yz(lax.rem(y + k, 4), z, core)
        return remote(by_set(y), by_set(y), bys.at[k], byr.at[k], seq, head)

    def by_wait(k):
        yf = lax.rem(y + 4 - k, 4)
        return remote(by_set(yf), by_set(yf), bys.at[k], byr.at[k], s, h)

    def fa_copy(o, c_):
        ref = wbuf.at[o // 4, :, lax.rem(o, 4), c_, :, LO]
        return remote(ref, ref, fas.at[o], far.at[o], sib, h)

    def fb_copy(y_, c_):
        ref = wbuf.at[:, y_, :, c_, :, HI]
        return remote(ref, ref, fbs.at[y_], fbr.at[y_], sib, h)

    for k in range(1, 4):
        ay_copy(k).start()
    seq_p, head_p = at_yz(y, lax.rem(z + 1, 8), core)
    seq_m, head_m = at_yz(y, lax.rem(z + 7, 8), core)
    bz_first_p = remote(
        wt_ref.at[:, HI], wbuf.at[zh, y, zl, core, :, HI], bzps.at[1], bzpr.at[1], seq_p, head_p
    )
    bz_first_m = remote(
        wt_ref.at[:, HI], wbuf.at[zh, y, zl, core, :, HI], bzms.at[1], bzmr.at[1], seq_m, head_m
    )
    bz_first_p.start()
    bz_first_m.start()

    def w_step(n):
        if n == 1:
            own_w.wait()
            for k in range(1, 4):
                ay_wait(k).wait_recv()
            zp_copy(1, 0, False).start()
            zm_copy(1, 0, False).start()
            fa_copy(z, core).start()
            zp_copy(1, 1, True).wait_recv()
            zp_copy(2, 1, False).start()
            zm_copy(1, 1, True).wait_recv()
            zm_copy(2, 1, False).start()
        if n == 2:
            zp_copy(1, 0, True).wait_recv()
            zp_copy(2, 0, False).start()
            zm_copy(1, 0, True).wait_recv()
            zm_copy(2, 0, False).start()
            fa_copy(lax.rem(z + 7, 8), core).start()
            fa_copy(lax.rem(z + 1, 8), core).start()
            zp_copy(2, 1, True).wait_recv()
            zp_copy(3, 1, False).start()
            zm_copy(2, 1, True).wait_recv()
            zm_copy(3, 1, False).start()
        if n == 3:
            zp_copy(3, 1, True).wait_recv()
            zp_copy(4, 1, False).start()
            zm_copy(3, 1, True).wait_recv()
            zp_copy(2, 0, True).wait_recv()
            zp_copy(3, 0, False).start()
            zm_copy(2, 0, True).wait_recv()
            zm_copy(3, 0, False).start()
            fa_copy(lax.rem(z + 6, 8), core).start()
            fa_copy(lax.rem(z + 2, 8), core).start()
        if n == 4:
            zp_copy(4, 1, True).wait_recv()
            for k in range(1, 4):
                by_copy(k).start()
            fb_copy(y, core).start()
        if n == 5:
            zp_copy(3, 0, True).wait_recv()
            zp_copy(4, 0, False).start()
            zm_copy(3, 0, True).wait_recv()
            fa_copy(lax.rem(z + 5, 8), core).start()
            fa_copy(lax.rem(z + 3, 8), core).start()
        if n == 6:
            zp_copy(4, 0, True).wait_recv()
            fa_copy(lax.rem(z + 4, 8), core).start()
            for k in range(1, 4):
                by_wait(k).wait_recv()
                fb_copy(lax.rem(y + 4 - k, 4), core).start()
        if n == 7:
            for o in range(8):
                fa_copy(o, 1 - core).wait_recv()
            for y_ in range(4):
                fb_copy(y_, 1 - core).wait_recv()

    kvbuf[0] = kv_ref[...]
    docbuf[0] = doc_ref[...]
    docq[core] = doc_ref[...]
    own_rows = pl.ds(core * ROWS, ROWS)
    for g in range(GROUP):
        q8[g, own_rows, :] = q_ref[:, g * HD:(g + 1) * HD]
        go8[g, own_rows, :] = go_ref[:, g * HD:(g + 1) * HD]
    for j in range(SPAN):
        mxb[j] = jnp.full((8, 2048), FLOOR, jnp.float32)
        lsb[j] = jnp.zeros((8, 2048), jnp.float32)
        dsb[j] = jnp.zeros((8, 2048), jnp.float32)

        @pl.when(chip < j)
        def _():
            kvbuf[j] = jnp.zeros((ROWS, 256), jnp.bfloat16)
            dsbuf[j] = jnp.zeros((ROWS, 2048), jnp.bfloat16)

    docq_wait.wait_recv()
    for g in range(GROUP):
        q_wait(g).wait_recv()
        go_wait(g).wait_recv()

    def forward(j, _):
        @pl.when(chip >= j)
        def _():
            @pl.when(j > 0)
            def _():
                doc_copy(j).wait_recv()
                kv_copy(j).wait_recv()

            ids = docbuf[j]
            drow = jnp.concatenate((docq[0], docq[1]), axis=1)
            low = jnp.zeros((1, 256), jnp.float32)
            for v in range(3):
                count = jnp.sum((ids == v).astype(jnp.float32), axis=1, keepdims=True)
                low = low + jnp.where(drow > v, count, 0.0)
            place = lax.broadcasted_iota(jnp.int32, (ROWS, 256), 0)
            token = lax.broadcasted_iota(jnp.int32, (ROWS, 256), 1)
            high = jnp.where(j == 0, token - core * ROWS, ROWS)
            keep = (place >= low.astype(jnp.int32)) & (place <= high)
            bias[...] = jnp.where(keep, 0.0, NEG)
            key_rows = kvbuf[j, :, :HD]
            value_rows = kvbuf[j, :, HD:]
            for g in range(GROUP):
                cols = slice(g * 256, (g + 1) * 256)
                logits = lax.dot_general(
                    key_rows, q8[g], NT, preferred_element_type=jnp.float32
                )
                grad_p = lax.dot_general(
                    value_rows, go8[g], NT, preferred_element_type=jnp.float32
                )
                logits = logits + bias[...]
                top = jnp.maximum(jnp.max(logits, axis=0, keepdims=True), FLOOR)
                weight = jnp.exp2((logits - top) * EXP_SCALE)
                ebuf[j, :, cols] = weight
                dpbuf[j, :, cols] = grad_p
                mxb[j, :, cols] = jnp.broadcast_to(top, (8, 256))
                lsb[j, :, cols] = jnp.sum(weight.reshape(16, 8, 256), axis=0)
                dsb[j, :, cols] = jnp.sum((weight * grad_p).reshape(16, 8, 256), axis=0)

        @pl.when(j == 4)
        def _():
            w_step(1)

        return 0

    lax.fori_loop(0, SPAN, forward, 0)
    w_step(2)

    top = mxb[0]
    for j in range(1, SPAN):
        top = jnp.maximum(top, mxb[j])
    total = jnp.zeros((8, 2048), jnp.float32)
    dots = jnp.zeros((8, 2048), jnp.float32)
    for j in range(SPAN):
        factor = jnp.exp2((mxb[j] - top) * EXP_SCALE)
        total = total + factor * lsb[j]
        dots = dots + factor * dsb[j]
    total = jnp.sum(total, axis=0, keepdims=True)
    dots = jnp.sum(dots, axis=0, keepdims=True)
    row = lax.broadcasted_iota(jnp.int32, (8, 2048), 0)
    stat[...] = jnp.where(row == 0, top, jnp.where(row == 1, total, dots))
    stat_copy = remote(stat, strecv, sts, str_, sib, h)
    stat_copy.start()
    stat_copy.wait_recv()
    m_own, m_far = stat[0:1], strecv[0:1]
    m_all = jnp.maximum(m_own, m_far)
    f_own = jnp.exp2((m_own - m_all) * EXP_SCALE)
    f_far = jnp.exp2((m_far - m_all) * EXP_SCALE)
    l_all = stat[1:2] * f_own + strecv[1:2] * f_far
    d_all = (stat[2:3] * f_own + strecv[2:3] * f_far) / l_all
    stat_copy.wait_send()
    stat[0:1] = m_all
    stat[1:2] = 1.0 / l_all
    stat[2:3] = d_all

    def dk_copy(j):
        return remote(
            sendbuf.at[j], dkvrecv.at[j], dks.at[j], dkr.at[j], lax.rem(s - 2 * j + 32, 32), h
        )

    def backward(i, _):
        j = SPAN - 1 - i

        @pl.when(chip >= j)
        def _():
            for g in range(GROUP):
                cols = slice(g * 256, (g + 1) * 256)
                factor = jnp.exp2((mxb[j, 0:1, cols] - stat[0:1, cols]) * EXP_SCALE)
                factor = factor * stat[1:2, cols]
                probs = ebuf[j, :, cols] * factor
                pbuf[:, cols] = probs.astype(jnp.bfloat16)
                grad_l = probs * (dpbuf[j, :, cols] - stat[2:3, cols])
                dsbuf[j, :, cols] = grad_l.astype(jnp.bfloat16)
            grad_k = jnp.dot(
                dsbuf[j], q8[...].reshape(2048, HD), preferred_element_type=jnp.float32
            )
            grad_v = jnp.dot(
                pbuf[...], go8[...].reshape(2048, HD), preferred_element_type=jnp.float32
            )
            grad_k = grad_k * SCALE
            ownbuf[:, :HD] = grad_k
            ownbuf[:, HD:] = grad_v

            @pl.when(j > 0)
            def _():
                sendbuf[j, :, :HD] = grad_k.astype(jnp.bfloat16)
                sendbuf[j, :, HD:] = grad_v.astype(jnp.bfloat16)
                dk_copy(j).start()

        @pl.when(i == 4)
        def _():
            w_step(3)

        return 0

    lax.fori_loop(0, SPAN, backward, 0)
    w_step(4)

    key_t = jnp.concatenate([jnp.transpose(kvbuf[j, :, :HD]) for j in range(SPAN)], axis=1)
    for g in range(GROUP):
        grad_t = jnp.dot(
            key_t,
            dsbuf[:, :, g * 256:(g + 1) * 256].reshape(SPAN * ROWS, 256),
            preferred_element_type=jnp.float32,
        )
        dqbuf[:, g * HD:(g + 1) * HD] = jnp.transpose(grad_t) * SCALE
    dq_copy = remote(dqbuf.at[pl.ds((1 - core) * ROWS, ROWS)], dqrecv, dqs, dqr, sib, h)
    dq_copy.start()
    w_step(5)

    acc = ownbuf[...]
    ownbuf[...] = acc
    for j in range(1, SPAN):

        @pl.when(chip + j <= 15)
        def _():
            dk_copy(j).wait_recv()
            ownbuf[...] += dkvrecv[j].astype(jnp.float32)

    grad_kv = ownbuf[...].astype(jnp.bfloat16)
    gkv_ref[...] = grad_kv
    gbuf[h] = grad_kv

    z_send = remote(gbuf.at[h], gbuf.at[h], g1s, g1r, s, x * 2 + 1 - zh)
    z_wait = remote(gbuf.at[h], gbuf.at[x * 2 + 1 - zh], g1s, g1r, s, x * 2 + 1 - zh)
    z_send.start()

    def gx_copy(k, far):
        hh = (x * 2 + 1 - zh) if far else h
        xt = lax.rem(x + k, 4)
        n = k + (4 if far else 0)
        return remote(gbuf.at[hh], gbuf.at[hh], gxs.at[n], gxr.at[n], s, xt * 2 + zh)

    def gx_wait(k, far):
        xf = lax.rem(x + 4 - k, 4)
        hh = xf * 2 + ((1 - zh) if far else zh)
        n = k + (4 if far else 0)
        return remote(gbuf.at[hh], gbuf.at[hh], gxs.at[n], gxr.at[n], s, h)

    for k in range(1, 4):
        gx_copy(k, False).start()
    dq_copy.wait_recv()
    gq_ref[...] = (dqbuf[own_rows, :] + dqrecv[...]).astype(jnp.bfloat16)
    z_wait.wait_recv()
    for k in range(1, 4):
        gx_copy(k, True).start()

    w_step(6)
    own_delta.wait()
    for k in range(1, 4):
        del_wait(k).wait_recv()
    w_step(7)

    def project(n, _):
        out = None
        for b in range(2):
            left = dbuf[:, :, b * 1024:(b + 1) * 1024].reshape(512, 1024)
            right = wbuf[b, n].reshape(512, 1024)
            part = lax.dot_general(left, right, NT, preferred_element_type=jnp.float32)
            out = part if out is None else out + part
        pbig[n] = out
        return 0

    lax.fori_loop(0, 4, project, 0)
    for k in range(1, 4):
        gx_wait(k, False).wait_recv()
        gx_wait(k, True).wait_recv()

    lane = lax.broadcasted_iota(jnp.int32, (8, 128), 1)
    sub = lax.broadcasted_iota(jnp.int32, (8, 128), 0)
    tile = jnp.zeros((8, 128), jnp.float32)
    for hh in range(8):
        grads = gbuf[hh].astype(jnp.float32)
        off = (hh % 2) * 256
        for i in range(4):
            prod = pbig[hh // 2, i * 128:(i + 1) * 128, off:off + 256] * grads
            prod = jnp.sum(prod.reshape(16, 8, 256), axis=0)
            prod = jnp.sum(prod, axis=0, keepdims=True)
            for n in range(2):
                value = jnp.sum(prod[:, n * 128:(n + 1) * 128], axis=1, keepdims=True)
                hit = (sub == 2 * i + zh) & (lane == 2 * hh + n)
                tile = jnp.where(hit, value, tile)
    tile = tile * (1.0 / 64.0)

    def reduce_over(tile, n, me, peer, buf, src, ss, rs):
        src[...] = tile
        buf[me] = tile
        for k in range(1, n):
            to = lax.rem(me + k, n)
            seq, head = peer(to)
            remote(src, buf.at[me], ss.at[k], rs.at[k], seq, head).start()
        for k in range(1, n):
            frm = lax.rem(me + n - k, n)
            remote(src, buf.at[frm], ss.at[k], rs.at[k], s, h).wait_recv()
        out = buf[0]
        for k in range(1, n):
            out = out + buf[k]
        return out

    tile = reduce_over(
        tile, 8, y * 2 + core, lambda t: at_yz(t // 2, z, lax.rem(t, 2)), ar1, arsrc.at[0], a1s, a1r
    )
    tile = reduce_over(tile, 8, z, lambda t: at_yz(y, t, core), ar2, arsrc.at[1], a2s, a2r)
    tile = reduce_over(tile, 4, x, lambda t: (s, t * 2 + zh), ar3, arsrc.at[2], a3s, a3r)
    sc_ref[...] = tile

    docq_send.wait_send()
    for g in range(GROUP):
        q_copy(g).wait_send()
        go_copy(g).wait_send()
    for j in range(1, SPAN):

        @pl.when(chip + j <= 15)
        def _():
            doc_copy(j).wait_send()
            kv_copy(j).wait_send()

        @pl.when(chip >= j)
        def _():
            dk_copy(j).wait_send()

    for k in range(1, 4):
        del_copy(k).wait_send()
        ay_copy(k).wait_send()
        by_copy(k).wait_send()
        gx_copy(k, False).wait_send()
        gx_copy(k, True).wait_send()
    for k in range(1, 5):
        for colour in range(2):
            zp_copy(k, colour, False).wait_send()
            if k < 4:
                zm_copy(k, colour, False).wait_send()
    for o in range(8):
        fa_copy(o, core).wait_send()
    for y_ in range(4):
        fb_copy(y_, core).wait_send()
    dq_copy.wait_send()
    z_send.wait_send()
    for n, src, buf, ss, rs in (
        (8, arsrc.at[0], ar1, a1s, a1r),
        (8, arsrc.at[1], ar2, a2s, a2r),
        (4, arsrc.at[2], ar3, a3s, a3r),
    ):
        for k in range(1, n):
            remote(src, buf.at[0], ss.at[k], rs.at[k], s, h).wait_send()


def on_device(queries, keyval, grad_out, doc_ids, deltas, node_weights, layer_slot):
    vmem = pl.BlockSpec(memory_space=pltpu.VMEM)
    hbm = pl.BlockSpec(memory_space=pl.ANY)
    bf, f32, i32 = jnp.bfloat16, jnp.float32, jnp.int32
    V, D = pltpu.VMEM, pltpu.SemaphoreType.DMA
    scratch = [
        V((8, 256, 128), bf),
        V((8, 256, 128), bf),
        V((SPAN, 128, 256), bf),
        V((SPAN, 1, 128), i32),
        V((2, 1, 128), i32),
        V((128, 256), f32),
        V((SPAN, 128, 2048), f32),
        V((SPAN, 128, 2048), f32),
        V((SPAN, 8, 2048), f32),
        V((SPAN, 8, 2048), f32),
        V((SPAN, 8, 2048), f32),
        V((8, 2048), f32),
        V((8, 2048), f32),
        V((128, 2048), bf),
        V((SPAN, 128, 2048), bf),
        V((SPAN, 128, 256), bf),
        V((SPAN, 128, 256), bf),
        V((128, 256), f32),
        V((256, 1024), f32),
        V((128, 1024), f32),
        V((4, 128, 2048), bf),
        V((2, 4, 4, 2, 64, 1024), bf),
        V((4, 512, 512), f32),
        V((8, 128, 256), bf),
        V((3, 8, 128), f32),
        V((8, 8, 128), f32),
        V((8, 8, 128), f32),
        V((4, 8, 128), f32),
    ]
    sems = [
        9, 9, 9, 9, 16, 16, None, None, 9, 9, None, None, 4, 4, 2,
        4, 4, 5, 5, 4, 4, 5, 5, 4, 4, 4, 4, 8, 8, 4, 4, None, None, 8, 8,
        8, 8, 8, 8, 4, 4,
    ]
    scratch += [D if n is None else D((n,)) for n in sems]
    grad_query, grad_keyval, tile = pl.pallas_call(
        kernel,
        out_shape=(
            jax.ShapeDtypeStruct((128, 1024), bf),
            jax.ShapeDtypeStruct((128, 256), bf),
            jax.ShapeDtypeStruct((8, 128), f32),
        ),
        in_specs=[vmem, vmem, vmem, vmem, hbm, vmem],
        out_specs=(vmem, vmem, vmem),
        scratch_shapes=scratch,
        compiler_params=pltpu.CompilerParams(
            has_side_effects=True, vmem_limit_bytes=60 * 1024 * 1024
        ),
    )(
        queries,
        keyval,
        grad_out,
        doc_ids.reshape(1, 128),
        deltas.reshape(128, 8192),
        node_weights.T,
    )
    placing = (layer_slot[:, None] == jnp.arange(8, dtype=jnp.int32)[None, :]).astype(f32)
    scores = jnp.dot(placing.T, tile[:, :16], precision=lax.Precision.HIGHEST)
    return (grad_query, grad_keyval, scores)


def solution(mesh):
    return jax.shard_map(
        on_device,
        mesh=mesh,
        in_specs=(
            P("seq", "head"),
            P("seq", "head"),
            P("seq", "head"),
            P("seq"),
            P("head", "seq", None),
            P("head", "seq"),
            P(),
        ),
        out_specs=(P("seq", "head"), P("seq", "head"), P()),
        check_vma=False,
    )
```

```python
import math

import jax
import jax.numpy as jnp
from jax import lax
from jax.experimental import pallas as pl
from jax.experimental.pallas import tpu as pltpu
from jax.sharding import PartitionSpec as P

HD = 128
GROUP = 8
ROWS = 128
SPAN = 9
CUT = 384
NEG = -1e30
FLOOR = -1e29
SCALE = 1.0 / math.sqrt(HD)
EXP_SCALE = SCALE * math.log2(math.e)
MESH = pl.DeviceIdType.MESH
NT = (((1,), (1,)), ((), ()))


def remote(src, dst, send, recv, seq, head):
    return pltpu.make_async_remote_copy(
        src_ref=src,
        dst_ref=dst,
        send_sem=send,
        recv_sem=recv,
        device_id=(seq, head),
        device_id_type=MESH,
    )


def kernel(
    q_ref,
    kv_ref,
    go_ref,
    doc_ref,
    del_ref,
    wt_ref,
    gq_ref,
    gkv_ref,
    sc_ref,
    q8,
    go8,
    kvbuf,
    docbuf,
    docq,
    bias,
    ebuf,
    dpbuf,
    mxb,
    lsb,
    dsb,
    stat,
    strecv,
    pbuf,
    dsbuf,
    sendbuf,
    dkvrecv,
    ownbuf,
    dqbuf,
    dqrecv,
    dbuf,
    wbuf,
    pbig,
    gbuf,
    arsrc,
    ar1,
    ar2,
    ar3,
    kvs,
    kvr,
    docs,
    docr,
    qs,
    qr,
    sts,
    str_,
    dks,
    dkr,
    dqs,
    dqr,
    dls,
    dlr,
    loc,
    ays,
    ayr,
    azs,
    azr,
    bzs,
    bzr,
    bys,
    byr,
    bos,
    bor,
    fs,
    fr,
    g1s,
    g1r,
    gxs,
    gxr,
    a1s,
    a1r,
    a2s,
    a2r,
    a3s,
    a3r,
):
    s = lax.axis_index("seq")
    h = lax.axis_index("head")
    core = lax.rem(s, 2)
    chip = s // 2
    zl = lax.rem(chip, 4)
    y = chip // 4
    zh = lax.rem(h, 2)
    x = h // 2
    z = zh * 4 + zl
    sib = s + 1 - 2 * core

    def at_yz(y_, z_, c_):
        return (y_ * 4 + lax.rem(z_, 4)) * 2 + c_, x * 2 + z_ // 4

    def kv_copy(j):
        return remote(kv_ref, kvbuf.at[j], kvs.at[j], kvr.at[j], lax.rem(s + 2 * j, 32), h)

    def doc_copy(j):
        return remote(doc_ref, docbuf.at[j], docs.at[j], docr.at[j], lax.rem(s + 2 * j, 32), h)

    def q_copy(g):
        return remote(
            q_ref.at[:, pl.ds(g * HD, HD)],
            q8.at[g, pl.ds(core * ROWS, ROWS)],
            qs.at[g],
            qr.at[g],
            sib,
            h,
        )

    def go_copy(g):
        return remote(
            go_ref.at[:, pl.ds(g * HD, HD)],
            go8.at[g, pl.ds(core * ROWS, ROWS)],
            qs.at[8 + g],
            qr.at[8 + g],
            sib,
            h,
        )

    def q_wait(g):
        return remote(
            q_ref.at[:, pl.ds(g * HD, HD)],
            q8.at[g, pl.ds((1 - core) * ROWS, ROWS)],
            qs.at[g],
            qr.at[g],
            sib,
            h,
        )

    def go_wait(g):
        return remote(
            go_ref.at[:, pl.ds(g * HD, HD)],
            go8.at[g, pl.ds((1 - core) * ROWS, ROWS)],
            qs.at[8 + g],
            qr.at[8 + g],
            sib,
            h,
        )

    barrier = pltpu.get_barrier_semaphore()

    def greet(seq, head):
        pl.semaphore_signal(barrier, inc=1, device_id=(seq, head), device_id_type=MESH)

    for k in range(1, 16):
        greet(lax.rem(s + 2 * k, 32), h)
    for k in range(4):
        greet(lax.rem(y + k, 4) * 8 + zl * 2 + 1 - core, h)
        greet(y * 8 + k * 2 + core, x * 2 + 1 - zh)
    for k in range(1, 4):
        greet(s, lax.rem(x + k, 4) * 2 + zh)
    pl.semaphore_wait(barrier, 26)

    docq_send = remote(doc_ref, docq.at[core], docs.at[0], docr.at[0], sib, h)
    docq_wait = remote(doc_ref, docq.at[1 - core], docs.at[0], docr.at[0], sib, h)
    docq_send.start()
    for j in range(1, SPAN):

        @pl.when(chip + j <= 15)
        def _():
            doc_copy(j).start()
            kv_copy(j).start()

    for g in range(GROUP):
        q_copy(g).start()
        go_copy(g).start()

    def del_copy(k):
        xt = lax.rem(x + k, 4)
        return remote(
            del_ref.at[:, pl.ds(xt * 2048, 2048)],
            dbuf.at[x],
            dls.at[k],
            dlr.at[k],
            s,
            xt * 2 + zh,
        )

    def del_wait(k):
        xf = lax.rem(x + 4 - k, 4)
        return remote(
            del_ref.at[:, pl.ds(xf * 2048, 2048)],
            dbuf.at[xf],
            dls.at[k],
            dlr.at[k],
            s,
            xf * 2 + zh,
        )

    for k in range(1, 4):
        del_copy(k).start()
    own_delta = pltpu.make_async_copy(
        del_ref.at[:, pl.ds(x * 2048, 2048)], dbuf.at[x], loc.at[0]
    )
    own_delta.start()

    LA, LB = pl.ds(0, CUT), pl.ds(CUT, 1024 - CUT)
    sent = {}

    def send(build, *args):
        build(*args).start()
        sent[(build, args)] = True

    def piece(r, m, lanes, c_=None):
        o = lax.rem(z + r, 8)
        return wbuf.at[
            o // 4, lax.rem(y + 4 - m, 4), lax.rem(o, 4), core if c_ is None else c_, :, lanes
        ]

    def to_y(k):
        return at_yz(lax.rem(y + k, 4), z, core)

    def to_z(d):
        return at_yz(y, lax.rem(z + d + 8, 8), core)

    def ay(k, wait=False):
        dst = piece(0, k if wait else 0, LA)
        return remote(wt_ref.at[:, LA], dst, ays.at[k], ayr.at[k], *to_y(k))

    def az(d, k, m, wait=False):
        ref = piece((-d * (k if wait else k - 1)) % 8, m, LA)
        src = wt_ref.at[:, LA] if (k == 1 and m == 0) else ref
        n = ((d < 0) * 5 + k) * 4 + m
        return remote(src, ref, azs.at[n], azr.at[n], *to_z(d))

    def bz(d, k, wait=False):
        ref = piece((-d * (k if wait else k - 1)) % 8, 0, LB)
        src = wt_ref.at[:, LB] if k == 1 else ref
        n = (d < 0) * 5 + k
        return remote(src, ref, bzs.at[n], bzr.at[n], *to_z(d))

    def by(d, r, wait=False):
        ref = piece(r, (d % 4) if wait else 0, LB)
        src = wt_ref.at[:, LB] if r == 0 else ref
        n = (d < 0) * 8 + r
        return remote(src, ref, bys.at[n], byr.at[n], *to_y(d % 4))

    def bo(d, r, wait=False):
        ref = piece(r, 2 if wait else d % 4, LB)
        return remote(ref, ref, bos.at[r], bor.at[r], *to_y(d % 4))

    def own_row():
        ref = wbuf.at[zh, y, zl, core]
        return remote(wt_ref, ref, fs.at[0], fr, sib, h)

    def fa(r, m):
        ref = piece(r, m, LA)
        return remote(ref, ref, fs.at[r * 4 + m], fr, sib, h)

    def fb(r, m):
        ref = piece(r, m, LB)
        return remote(ref, ref, fs.at[32 + r * 4 + m], fr, sib, h)

    own_w = pltpu.make_async_copy(wt_ref, wbuf.at[zh, y, zl, core], loc.at[1])
    own_w.start()
    for d in (1, -1):
        send(bz, d, 1)
    for k in (1, 3, 2):
        send(ay, k)
    for d in (1, -1):
        send(az, d, 1, 0)
        send(by, d, 0)
    send(own_row)
    STEPS = {1: 4, -1: 3}

    def a_ring(k, ms):
        for m in ms:
            for d in (1, -1):
                if k <= STEPS[d]:
                    az(d, k, m, True).wait_recv()
                    if k < STEPS[d]:
                        send(az, d, k + 1, m)
                    send(fa, (-d * k) % 8, m)

    def b_ring(k):
        for d in (1, -1):
            if k <= STEPS[d]:
                bz(d, k, True).wait_recv()
                if k < STEPS[d]:
                    send(bz, d, k + 1)
                r = (-d * k) % 8
                send(by, 1, r)
                send(by, -1, r)
                send(fb, r, 0)

    def b_side(k):
        for r in sorted({k, -k % 8}):
            for d in (1, -1):
                by(d, r, True).wait_recv()
                if (d > 0) == (r < 4):
                    send(bo, d, r)
                send(fb, r, d % 4)

    def b_far(k):
        for r in sorted({k, -k % 8}):
            bo(1 if r < 4 else -1, r, True).wait_recv()
            send(fb, r, 2)

    def w_step(n):
        if n == 1:
            b_ring(1)
            for k in (1, 3, 2):
                ay(k, True).wait_recv()
                send(az, 1, 1, k)
                send(az, -1, 1, k)
                send(fa, 0, k)
            a_ring(1, (0,))
            b_side(0)
        if n == 2:
            b_ring(2)
            a_ring(1, (1, 3, 2))
            b_side(1)
            b_far(0)
        if n == 3:
            b_ring(3)
            a_ring(2, (0, 1, 3, 2))
            b_side(2)
            b_far(1)
        if n == 4:
            b_ring(4)
            a_ring(3, (0, 1, 3, 2))
            b_side(3)
            b_far(2)
        if n == 5:
            a_ring(4, (0, 1, 3, 2))
            b_side(4)
            b_far(3)
        if n == 6:
            b_far(4)
        if n == 7:
            own_w.wait()
            far = wbuf.at[:, :, :, 1 - core]
            remote(far, far, fs.at[0], fr, sib, h).wait_recv()

    kvbuf[0] = kv_ref[...]
    docbuf[0] = doc_ref[...]
    docq[core] = doc_ref[...]
    own_rows = pl.ds(core * ROWS, ROWS)
    for g in range(GROUP):
        q8[g, own_rows, :] = q_ref[:, g * HD:(g + 1) * HD]
        go8[g, own_rows, :] = go_ref[:, g * HD:(g + 1) * HD]
    for j in range(SPAN):

        @pl.when(chip < j)
        def _():
            mxb[j] = jnp.full((8, 2048), FLOOR, jnp.float32)
            lsb[j] = jnp.zeros((8, 2048), jnp.float32)
            dsb[j] = jnp.zeros((8, 2048), jnp.float32)
            kvbuf[j] = jnp.zeros((ROWS, 256), jnp.bfloat16)
            dsbuf[j] = jnp.zeros((ROWS, 2048), jnp.bfloat16)

    docq_wait.wait_recv()
    for g in range(GROUP):
        q_wait(g).wait_recv()
        go_wait(g).wait_recv()

    def forward(j, _):
        @pl.when(chip >= j)
        def _():
            @pl.when(j > 0)
            def _():
                doc_copy(j).wait_recv()
                kv_copy(j).wait_recv()

            ids = docbuf[j]
            drow = jnp.concatenate((docq[0], docq[1]), axis=1)
            low = jnp.zeros((1, 256), jnp.float32)
            for v in range(3):
                count = jnp.sum((ids == v).astype(jnp.float32), axis=1, keepdims=True)
                low = low + jnp.where(drow > v, count, 0.0)
            place = lax.broadcasted_iota(jnp.int32, (ROWS, 256), 0)
            token = lax.broadcasted_iota(jnp.int32, (ROWS, 256), 1)
            high = jnp.where(j == 0, token - core * ROWS, ROWS)
            keep = (place >= low.astype(jnp.int32)) & (place <= high)
            bias[...] = jnp.where(keep, 0.0, NEG)
            key_rows = kvbuf[j, :, :HD]
            value_rows = kvbuf[j, :, HD:]
            for g in range(GROUP):
                cols = slice(g * 256, (g + 1) * 256)
                logits = lax.dot_general(
                    key_rows, q8[g], NT, preferred_element_type=jnp.float32
                )
                grad_p = lax.dot_general(
                    value_rows, go8[g], NT, preferred_element_type=jnp.float32
                )
                logits = logits + bias[...]
                top = jnp.maximum(jnp.max(logits, axis=0, keepdims=True), FLOOR)
                weight = jnp.exp2((logits - top) * EXP_SCALE)
                ebuf[j, :, cols] = weight
                dpbuf[j, :, cols] = grad_p
                mxb[j, :, cols] = jnp.broadcast_to(top, (8, 256))
                lsb[j, :, cols] = jnp.sum(weight.reshape(16, 8, 256), axis=0)
                dsb[j, :, cols] = jnp.sum((weight * grad_p).reshape(16, 8, 256), axis=0)

        @pl.when(j == 5)
        def _():
            w_step(1)

        return 0

    lax.fori_loop(0, SPAN, forward, 0)

    top = mxb[0]
    for j in range(1, SPAN):
        top = jnp.maximum(top, mxb[j])
    total = jnp.zeros((8, 2048), jnp.float32)
    dots = jnp.zeros((8, 2048), jnp.float32)
    for j in range(SPAN):
        factor = jnp.exp2((mxb[j] - top) * EXP_SCALE)
        total = total + factor * lsb[j]
        dots = dots + factor * dsb[j]
    total = jnp.sum(total, axis=0, keepdims=True)
    dots = jnp.sum(dots, axis=0, keepdims=True)
    row = lax.broadcasted_iota(jnp.int32, (8, 2048), 0)
    stat[...] = jnp.where(row == 0, top, jnp.where(row == 1, total, dots))
    stat_copy = remote(stat, strecv, sts, str_, sib, h)
    stat_copy.start()
    stat_copy.wait_recv()
    m_own, m_far = stat[0:1], strecv[0:1]
    m_all = jnp.maximum(m_own, m_far)
    f_own = jnp.exp2((m_own - m_all) * EXP_SCALE)
    f_far = jnp.exp2((m_far - m_all) * EXP_SCALE)
    l_all = stat[1:2] * f_own + strecv[1:2] * f_far
    d_all = (stat[2:3] * f_own + strecv[2:3] * f_far) / l_all
    stat_copy.wait_send()
    stat[0:1] = m_all
    stat[1:2] = 1.0 / l_all
    stat[2:3] = d_all

    def dk_copy(j):
        return remote(
            sendbuf.at[j], dkvrecv.at[j], dks.at[j], dkr.at[j], lax.rem(s - 2 * j + 32, 32), h
        )

    def backward(i, _):
        j = SPAN - 1 - i

        @pl.when(chip >= j)
        def _():
            for g in range(GROUP):
                cols = slice(g * 256, (g + 1) * 256)
                factor = jnp.exp2((mxb[j, 0:1, cols] - stat[0:1, cols]) * EXP_SCALE)
                factor = factor * stat[1:2, cols]
                probs = ebuf[j, :, cols] * factor
                pbuf[:, cols] = probs.astype(jnp.bfloat16)
                grad_l = probs * (dpbuf[j, :, cols] - stat[2:3, cols])
                dsbuf[j, :, cols] = grad_l.astype(jnp.bfloat16)
            grad_k = jnp.dot(
                dsbuf[j], q8[...].reshape(2048, HD), preferred_element_type=jnp.float32
            )
            grad_v = jnp.dot(
                pbuf[...], go8[...].reshape(2048, HD), preferred_element_type=jnp.float32
            )
            grad_k = grad_k * SCALE
            ownbuf[:, :HD] = grad_k
            ownbuf[:, HD:] = grad_v

            @pl.when(j > 0)
            def _():
                sendbuf[j, :, :HD] = grad_k.astype(jnp.bfloat16)
                sendbuf[j, :, HD:] = grad_v.astype(jnp.bfloat16)
                dk_copy(j).start()

        @pl.when(i == 4)
        def _():
            w_step(2)

        return 0

    lax.fori_loop(0, SPAN, backward, 0)

    key_t = jnp.concatenate([jnp.transpose(kvbuf[j, :, :HD]) for j in range(SPAN)], axis=1)
    for g in range(GROUP):
        grad_t = jnp.dot(
            key_t,
            dsbuf[:, :, g * 256:(g + 1) * 256].reshape(SPAN * ROWS, 256),
            preferred_element_type=jnp.float32,
        )
        dqbuf[:, g * HD:(g + 1) * HD] = jnp.transpose(grad_t) * SCALE
    dq_copy = remote(dqbuf.at[pl.ds((1 - core) * ROWS, ROWS)], dqrecv, dqs, dqr, sib, h)
    dq_copy.start()
    w_step(3)

    acc = ownbuf[...]
    ownbuf[...] = acc
    for j in range(1, SPAN):

        @pl.when(chip + j <= 15)
        def _():
            dk_copy(j).wait_recv()
            ownbuf[...] += dkvrecv[j].astype(jnp.float32)

    grad_kv = ownbuf[...].astype(jnp.bfloat16)
    gkv_ref[...] = grad_kv
    gbuf[h] = grad_kv

    z_send = remote(gbuf.at[h], gbuf.at[h], g1s, g1r, s, x * 2 + 1 - zh)
    z_wait = remote(gbuf.at[h], gbuf.at[x * 2 + 1 - zh], g1s, g1r, s, x * 2 + 1 - zh)
    z_send.start()

    def gx_copy(k, far):
        hh = (x * 2 + 1 - zh) if far else h
        xt = lax.rem(x + k, 4)
        n = k + (4 if far else 0)
        return remote(gbuf.at[hh], gbuf.at[hh], gxs.at[n], gxr.at[n], s, xt * 2 + zh)

    def gx_wait(k, far):
        xf = lax.rem(x + 4 - k, 4)
        hh = xf * 2 + ((1 - zh) if far else zh)
        n = k + (4 if far else 0)
        return remote(gbuf.at[hh], gbuf.at[hh], gxs.at[n], gxr.at[n], s, h)

    for k in range(1, 4):
        gx_copy(k, False).start()
    w_step(4)
    dq_copy.wait_recv()
    gq_ref[...] = (dqbuf[own_rows, :] + dqrecv[...]).astype(jnp.bfloat16)
    w_step(5)
    z_wait.wait_recv()
    for k in range(1, 4):
        gx_copy(k, True).start()
    w_step(6)

    own_delta.wait()
    for k in range(1, 4):
        del_wait(k).wait_recv()
    w_step(7)

    def project(n, _):
        out = None
        for b in range(2):
            left = dbuf[:, :, b * 1024:(b + 1) * 1024].reshape(512, 1024)
            right = wbuf[b, n].reshape(512, 1024)
            part = lax.dot_general(left, right, NT, preferred_element_type=jnp.float32)
            out = part if out is None else out + part
        pbig[n] = out
        return 0

    lax.fori_loop(0, 4, project, 0)
    for k in range(1, 4):
        gx_wait(k, False).wait_recv()
        gx_wait(k, True).wait_recv()

    lane = lax.broadcasted_iota(jnp.int32, (8, 128), 1)
    sub = lax.broadcasted_iota(jnp.int32, (8, 128), 0)
    tile = jnp.zeros((8, 128), jnp.float32)
    for hh in range(8):
        grads = gbuf[hh].astype(jnp.float32)
        off = (hh % 2) * 256
        for i in range(4):
            prod = pbig[hh // 2, i * 128:(i + 1) * 128, off:off + 256] * grads
            prod = jnp.sum(prod.reshape(16, 8, 256), axis=0)
            prod = jnp.sum(prod, axis=0, keepdims=True)
            for n in range(2):
                value = jnp.sum(prod[:, n * 128:(n + 1) * 128], axis=1, keepdims=True)
                hit = (sub == 2 * i + zh) & (lane == 2 * hh + n)
                tile = jnp.where(hit, value, tile)
    tile = tile * (1.0 / 64.0)

    def reduce_over(tile, n, me, peer, buf, src, ss, rs):
        src[...] = tile
        buf[me] = tile
        for k in range(1, n):
            to = lax.rem(me + k, n)
            seq, head = peer(to)
            remote(src, buf.at[me], ss.at[k], rs.at[k], seq, head).start()
        for k in range(1, n):
            frm = lax.rem(me + n - k, n)
            remote(src, buf.at[frm], ss.at[k], rs.at[k], s, h).wait_recv()
        out = buf[0]
        for k in range(1, n):
            out = out + buf[k]
        return out

    tile = reduce_over(
        tile, 8, y * 2 + core, lambda t: at_yz(t // 2, z, lax.rem(t, 2)), ar1, arsrc.at[0], a1s, a1r
    )
    tile = reduce_over(tile, 8, z, lambda t: at_yz(y, t, core), ar2, arsrc.at[1], a2s, a2r)
    tile = reduce_over(tile, 4, x, lambda t: (s, t * 2 + zh), ar3, arsrc.at[2], a3s, a3r)
    sc_ref[...] = tile

    docq_send.wait_send()
    for g in range(GROUP):
        q_copy(g).wait_send()
        go_copy(g).wait_send()
    for j in range(1, SPAN):

        @pl.when(chip + j <= 15)
        def _():
            doc_copy(j).wait_send()
            kv_copy(j).wait_send()

        @pl.when(chip >= j)
        def _():
            dk_copy(j).wait_send()

    for k in range(1, 4):
        del_copy(k).wait_send()
        gx_copy(k, False).wait_send()
        gx_copy(k, True).wait_send()
    for build, args in sent:
        build(*args).wait_send()
    dq_copy.wait_send()
    z_send.wait_send()
    for n, src, buf, ss, rs in (
        (8, arsrc.at[0], ar1, a1s, a1r),
        (8, arsrc.at[1], ar2, a2s, a2r),
        (4, arsrc.at[2], ar3, a3s, a3r),
    ):
        for k in range(1, n):
            remote(src, buf.at[0], ss.at[k], rs.at[k], s, h).wait_send()


def finish(gq_in, gkv_in, tile_in, slot_ref, gq_out, gkv_out, sc_out):
    gq_out[...] = gq_in[...]
    gkv_out[...] = gkv_in[...]
    tile = tile_in[...]
    sub = lax.broadcasted_iota(jnp.int32, (8, 128), 0)
    scores = jnp.zeros((8, 128), jnp.float32)
    for i in range(8):
        scores = jnp.where(sub == slot_ref[i], tile[i:i + 1], scores)
    sc_out[...] = scores[:, :16]


def on_device(queries, keyval, grad_out, doc_ids, deltas, node_weights, layer_slot):
    vmem = pl.BlockSpec(memory_space=pltpu.VMEM)
    hbm = pl.BlockSpec(memory_space=pl.ANY)
    bf, f32, i32 = jnp.bfloat16, jnp.float32, jnp.int32
    V, D = pltpu.VMEM, pltpu.SemaphoreType.DMA
    scratch = [
        V((8, 256, 128), bf),
        V((8, 256, 128), bf),
        V((SPAN, 128, 256), bf),
        V((SPAN, 1, 128), i32),
        V((2, 1, 128), i32),
        V((128, 256), f32),
        V((SPAN, 128, 2048), f32),
        V((SPAN, 128, 2048), f32),
        V((SPAN, 8, 2048), f32),
        V((SPAN, 8, 2048), f32),
        V((SPAN, 8, 2048), f32),
        V((8, 2048), f32),
        V((8, 2048), f32),
        V((128, 2048), bf),
        V((SPAN, 128, 2048), bf),
        V((SPAN, 128, 256), bf),
        V((SPAN, 128, 256), bf),
        V((128, 256), f32),
        V((256, 1024), f32),
        V((128, 1024), f32),
        V((4, 128, 2048), bf),
        V((2, 4, 4, 2, 64, 1024), bf),
        V((4, 512, 512), f32),
        V((8, 128, 256), bf),
        V((3, 8, 128), f32),
        V((8, 8, 128), f32),
        V((8, 8, 128), f32),
        V((4, 8, 128), f32),
    ]
    sems = [
        9, 9, 9, 9, 16, 16, None, None, 9, 9, None, None, 4, 4, 2,
        4, 4, 40, 40, 10, 10, 16, 16, 8, 8, 64, None, None, None, 8, 8,
        8, 8, 8, 8, 4, 4,
    ]
    scratch += [D if n is None else D((n,)) for n in sems]
    grad_query, grad_keyval, tile = pl.pallas_call(
        kernel,
        out_shape=(
            jax.ShapeDtypeStruct((128, 1024), bf),
            jax.ShapeDtypeStruct((128, 256), bf),
            jax.ShapeDtypeStruct((8, 128), f32),
        ),
        in_specs=[vmem, vmem, vmem, vmem, hbm, vmem],
        out_specs=(vmem, vmem, vmem),
        scratch_shapes=scratch,
        compiler_params=pltpu.CompilerParams(
            has_side_effects=True, collective_id=0, vmem_limit_bytes=60 * 1024 * 1024
        ),
    )(
        queries,
        keyval,
        grad_out,
        doc_ids.reshape(1, 128),
        deltas.reshape(128, 8192),
        node_weights.T,
    )
    return pl.pallas_call(
        finish,
        out_shape=(
            jax.ShapeDtypeStruct((128, 1024), bf),
            jax.ShapeDtypeStruct((128, 256), bf),
            jax.ShapeDtypeStruct((8, 16), f32),
        ),
        in_specs=[vmem, vmem, vmem, pl.BlockSpec(memory_space=pltpu.SMEM)],
        out_specs=(vmem, vmem, vmem),
    )(grad_query, grad_keyval, tile, layer_slot)


def solution(mesh):
    return jax.shard_map(
        on_device,
        mesh=mesh,
        in_specs=(
            P("seq", "head"),
            P("seq", "head"),
            P("seq", "head"),
            P("seq"),
            P("head", "seq", None),
            P("head", "seq"),
            P(),
        ),
        out_specs=(P("seq", "head"), P("seq", "head"), P()),
        check_vma=False,
    )
```

```python
import math

import jax
import jax.numpy as jnp
from jax import lax
from jax.experimental import pallas as pl
from jax.experimental.pallas import tpu as pltpu
from jax.sharding import PartitionSpec as P

HD = 128
GROUP = 8
ROWS = 128
SPAN = 9
CUT = 16
FORWARD_STEPS = ((1, (0, 1)), (3, (2, 3)), (5, (4, 5)), (7, (6,)))
STEPS_1, STEPS_2, STEPS_3, STEPS_4, STEPS_5, STEPS_6 = (7, 8), (9,), (), (10, 11), (), (12,)
NEG = -1e30
FLOOR = -1e29
SCALE = 1.0 / math.sqrt(HD)
EXP_SCALE = SCALE * math.log2(math.e)
MESH = pl.DeviceIdType.MESH
NT = (((1,), (1,)), ((), ()))


def remote(src, dst, send, recv, seq, head):
    return pltpu.make_async_remote_copy(
        src_ref=src,
        dst_ref=dst,
        send_sem=send,
        recv_sem=recv,
        device_id=(seq, head),
        device_id_type=MESH,
    )


def kernel(
    q_ref,
    kv_ref,
    go_ref,
    doc_ref,
    del_ref,
    wt_ref,
    gq_ref,
    gkv_ref,
    sc_ref,
    qall,
    goall,
    kvbuf,
    docbuf,
    docq,
    bias,
    ebuf,
    dpbuf,
    mxb,
    lsb,
    dsb,
    stat,
    strecv,
    pbuf,
    dsbuf,
    sendbuf,
    dkvrecv,
    ownbuf,
    dqbuf,
    gqbuf,
    dqrecv,
    dbuf,
    wbuf,
    pbig,
    gbuf,
    arsrc,
    ar1,
    ar2,
    kvs,
    kvr,
    docs,
    docr,
    qs,
    qr,
    sts,
    str_,
    dks,
    dkr,
    dqs,
    dqr,
    dls,
    dlr,
    loc,
    ays,
    ayr,
    azs,
    azr,
    bzs,
    bzr,
    bys,
    byr,
    bos,
    bor,
    fs,
    fr,
    g1s,
    g1r,
    gxs,
    gxr,
    a1s,
    a1r,
    a2s,
    a2r,
):
    s = lax.axis_index("seq")
    h = lax.axis_index("head")
    core = lax.rem(s, 2)
    chip = s // 2
    zl = lax.rem(chip, 4)
    y = chip // 4
    zh = lax.rem(h, 2)
    x = h // 2
    z = zh * 4 + zl
    sib = s + 1 - 2 * core

    def at_yz(y_, z_, c_):
        return (y_ * 4 + lax.rem(z_, 4)) * 2 + c_, x * 2 + z_ // 4

    def kv_copy(j):
        return remote(kv_ref, kvbuf.at[j], kvs.at[j], kvr.at[j], lax.rem(s + 2 * j, 32), h)

    def doc_copy(j):
        return remote(doc_ref, docbuf.at[j], docs.at[j], docr.at[j], lax.rem(s + 2 * j, 32), h)

    own_rows = pl.ds(core * ROWS, ROWS)
    far_rows = pl.ds((1 - core) * ROWS, ROWS)
    q_copy = remote(q_ref, qall.at[own_rows], qs.at[0], qr.at[0], sib, h)
    q_wait = remote(q_ref, qall.at[far_rows], qs.at[0], qr.at[0], sib, h)
    go_copy = remote(go_ref, goall.at[own_rows], qs.at[1], qr.at[1], sib, h)
    go_wait = remote(go_ref, goall.at[far_rows], qs.at[1], qr.at[1], sib, h)
    own = [
        pltpu.make_async_copy(src, dst, loc.at[2 + n])
        for n, (src, dst) in enumerate(
            (
                (q_ref, qall.at[own_rows]),
                (go_ref, goall.at[own_rows]),
                (kv_ref, kvbuf.at[0]),
                (doc_ref, docbuf.at[0]),
                (doc_ref, docq.at[core]),
            )
        )
    ]
    for copy in own:
        copy.start()

    barrier = pltpu.get_barrier_semaphore()

    def greet(seq, head):
        pl.semaphore_signal(barrier, inc=1, device_id=(seq, head), device_id_type=MESH)

    for k in range(1, 16):
        greet(lax.rem(s + 2 * k, 32), h)
    for k in range(4):
        greet(lax.rem(y + k, 4) * 8 + zl * 2 + 1 - core, h)
        greet(y * 8 + k * 2 + core, x * 2 + 1 - zh)
    for k in range(1, 4):
        for n in range(4):
            for c_ in range(2):
                greet((n * 4 + zl) * 2 + c_, lax.rem(x + k, 4) * 2 + zh)
    pl.semaphore_wait(barrier, 47)

    LA, LB = pl.ds(0, CUT), pl.ds(CUT, 64 - CUT)
    sent = {}

    def send(build, *args):
        build(*args).start()
        sent[(build, args)] = True

    def piece(r, m, rows, c_=None):
        o = lax.rem(z + r, 8)
        return wbuf.at[
            o // 4, lax.rem(y + 4 - m, 4), lax.rem(o, 4), core if c_ is None else c_, rows
        ]

    def to_y(k):
        return at_yz(lax.rem(y + k, 4), z, core)

    def to_z(d):
        return at_yz(y, lax.rem(z + d + 8, 8), core)

    def ay(k, wait=False):
        dst = piece(0, k if wait else 0, LA)
        return remote(wt_ref.at[LA], dst, ays.at[k], ayr.at[k], *to_y(k))

    def az(d, k, half, wait=False):
        o = lax.rem(z + (-d * (k if wait else k - 1)) % 8, 8)
        ref = wbuf.at[o // 4, pl.ds(half * 2, 2), lax.rem(o, 4), core, LA]
        n = ((d < 0) * 5 + k) * 2 + half
        return remote(ref, ref, azs.at[n], azr.at[n], *to_z(d))

    def bz(d, k, wait=False):
        ref = piece((-d * (k if wait else k - 1)) % 8, 0, LB)
        src = wt_ref.at[LB] if k == 1 else ref
        n = (d < 0) * 5 + k
        return remote(src, ref, bzs.at[n], bzr.at[n], *to_z(d))

    def by(d, r, wait=False):
        ref = piece(r, (d % 4) if wait else 0, LB)
        src = wt_ref.at[LB] if r == 0 else ref
        n = (d < 0) * 8 + r
        return remote(src, ref, bys.at[n], byr.at[n], *to_y(d % 4))

    def bo(d, r, wait=False):
        ref = piece(r, 2 if wait else d % 4, LB)
        return remote(ref, ref, bos.at[r], bor.at[r], *to_y(d % 4))

    def fa(r):
        o = lax.rem(z + r, 8)
        ref = wbuf.at[o // 4, :, lax.rem(o, 4), core, LA]
        return remote(ref, ref, fs.at[r], fr.at[0], sib, h)

    def fb(m):
        ref = wbuf.at[:, lax.rem(y + 4 - m, 4), :, core, LB]
        return remote(ref, ref, fs.at[8 + m], fr.at[1 + m // 2 + m % 2], sib, h)

    def fb_one(r):
        ref = piece(r, 2, LB)
        return remote(ref, ref, fs.at[16 + r], fr.at[4], sib, h)

    own_w = pltpu.make_async_copy(wt_ref, wbuf.at[zh, y, zl, core], loc.at[1])
    own_w.start()
    for d in (1, -1):
        send(bz, d, 1)
    for k in (1, 3, 2):
        send(ay, k)
    for d in (1, -1):
        send(by, d, 0)
    STEPS = {1: 4, -1: 3}

    def a_ring(k):
        for half in range(2):
            for d in (1, -1):
                if k <= STEPS[d]:
                    az(d, k, half, True).wait_recv()
                    if k < STEPS[d]:
                        send(az, d, k + 1, half)
        for r in sorted({k, -k % 8}):
            send(fa, r)

    def b_ring(k):
        for d in (1, -1):
            if k <= STEPS[d]:
                bz(d, k, True).wait_recv()
                if k < STEPS[d]:
                    send(bz, d, k + 1)
                r = (-d * k) % 8
                send(by, 1, r)
                send(by, -1, r)
        if k == 4:
            send(fb, 0)

    def b_side(k):
        for r in sorted({k, -k % 8}):
            for d in (1, -1):
                by(d, r, True).wait_recv()
                if (d > 0) == (r < 4):
                    send(bo, d, r)
        if k == 4:
            send(fb, 1)
            send(fb, 3)

    def b_far(k):
        for r in sorted({k, -k % 8}):
            bo(1 if r < 4 else -1, r, True).wait_recv()
            send(fb_one, r)

    def a_side():
        own_w.wait()
        for k in (1, 3, 2):
            ay(k, True).wait_recv()
        for half in range(2):
            send(az, 1, 1, half)
            send(az, -1, 1, half)
        send(fa, 0)

    plan = (
        ((b_ring, 1), (a_side,)),
        ((b_side, 0),),
        ((b_ring, 2),),
        ((a_ring, 1),),
        ((b_side, 1), (b_far, 0)),
        ((b_ring, 3),),
        ((a_ring, 2),),
        ((b_side, 2), (b_far, 1)),
        ((b_ring, 4),),
        ((a_ring, 3),),
        ((b_side, 3), (b_far, 2)),
        ((a_ring, 4), (b_side, 4), (b_far, 3)),
        ((b_far, 4),),
    )

    def w_step(*ns):
        for n in ns:
            for job in plan[n]:
                job[0](*job[1:])

    def w_near():
        ref = wbuf.at[:, :, :, 1 - core, LA]
        remote(ref, ref, fs.at[0], fr.at[0], sib, h).wait_recv()
        for m in (0, 1, 3):
            ref = wbuf.at[:, lax.rem(y + 4 - m, 4), :, 1 - core, LB]
            remote(ref, ref, fs.at[0], fr.at[1 + m // 2 + m % 2], sib, h).wait_recv()

    def w_far():
        ref = wbuf.at[:, lax.rem(y + 2, 4), :, 1 - core, LB]
        remote(ref, ref, fs.at[0], fr.at[4], sib, h).wait_recv()

    docq_send = remote(doc_ref, docq.at[core], docs.at[0], docr.at[0], sib, h)
    docq_wait = remote(doc_ref, docq.at[1 - core], docs.at[0], docr.at[0], sib, h)
    docq_send.start()
    for j in range(1, SPAN):

        @pl.when(chip + j <= 15)
        def _():
            doc_copy(j).start()
            kv_copy(j).start()

    q_copy.start()
    go_copy.start()

    def del_copy(k):
        xt = lax.rem(x + k, 4)
        return remote(
            del_ref.at[:, pl.ds(xt * 2048, 2048)],
            dbuf.at[x],
            dls.at[k],
            dlr.at[k],
            s,
            xt * 2 + zh,
        )

    def del_wait(k):
        xf = lax.rem(x + 4 - k, 4)
        return remote(
            del_ref.at[:, pl.ds(xf * 2048, 2048)],
            dbuf.at[xf],
            dls.at[k],
            dlr.at[k],
            s,
            xf * 2 + zh,
        )

    for k in range(1, 4):
        del_copy(k).start()
    own_delta = pltpu.make_async_copy(
        del_ref.at[:, pl.ds(x * 2048, 2048)], dbuf.at[x], loc.at[0]
    )
    own_delta.start()

    for j in range(SPAN):

        @pl.when(chip < j)
        def _():
            mxb[j] = jnp.full((8, 2048), FLOOR, jnp.float32)
            lsb[j] = jnp.zeros((8, 2048), jnp.float32)
            dsb[j] = jnp.zeros((8, 2048), jnp.float32)
            kvbuf[j] = jnp.zeros((ROWS, 256), jnp.bfloat16)
            dsbuf[j] = jnp.zeros((ROWS, 2048), jnp.bfloat16)

    for copy in own:
        copy.wait()
    docq_wait.wait_recv()
    q_wait.wait_recv()
    go_wait.wait_recv()

    def forward(j, _):
        @pl.when(chip >= j)
        def _():
            @pl.when(j > 0)
            def _():
                doc_copy(j).wait_recv()
                kv_copy(j).wait_recv()

            ids = docbuf[j]
            drow = jnp.concatenate((docq[0], docq[1]), axis=1)
            low = jnp.zeros((1, 256), jnp.float32)
            for v in range(3):
                count = jnp.sum((ids == v).astype(jnp.float32), axis=1, keepdims=True)
                low = low + jnp.where(drow > v, count, 0.0)
            place = lax.broadcasted_iota(jnp.int32, (ROWS, 256), 0)
            token = lax.broadcasted_iota(jnp.int32, (ROWS, 256), 1)
            high = jnp.where(j == 0, token - core * ROWS, ROWS)
            keep = (place >= low.astype(jnp.int32)) & (place <= high)
            bias[...] = jnp.where(keep, 0.0, NEG)
            key_rows = kvbuf[j, :, :HD]
            value_rows = kvbuf[j, :, HD:]
            for g in range(GROUP):
                cols = slice(g * 256, (g + 1) * 256)
                logits = lax.dot_general(
                    key_rows, qall[:, g * HD:(g + 1) * HD], NT, preferred_element_type=jnp.float32
                )
                grad_p = lax.dot_general(
                    value_rows, goall[:, g * HD:(g + 1) * HD], NT, preferred_element_type=jnp.float32
                )
                logits = logits + bias[...]
                top = jnp.maximum(jnp.max(logits, axis=0, keepdims=True), FLOOR)
                weight = jnp.exp2((logits - top) * EXP_SCALE)
                ebuf[j, :, cols] = weight
                dpbuf[j, :, cols] = grad_p
                mxb[j, :, cols] = jnp.broadcast_to(top, (8, 256))
                lsb[j, :, cols] = jnp.sum(weight.reshape(16, 8, 256), axis=0)
                dsb[j, :, cols] = jnp.sum((weight * grad_p).reshape(16, 8, 256), axis=0)

        for n, ns in FORWARD_STEPS:

            @pl.when(j == n)
            def _():
                w_step(*ns)

        return 0

    lax.fori_loop(0, SPAN, forward, 0)

    top = mxb[0]
    for j in range(1, SPAN):
        top = jnp.maximum(top, mxb[j])
    total = jnp.zeros((8, 2048), jnp.float32)
    dots = jnp.zeros((8, 2048), jnp.float32)
    for j in range(SPAN):
        factor = jnp.exp2((mxb[j] - top) * EXP_SCALE)
        total = total + factor * lsb[j]
        dots = dots + factor * dsb[j]
    total = jnp.sum(total, axis=0, keepdims=True)
    dots = jnp.sum(dots, axis=0, keepdims=True)
    row = lax.broadcasted_iota(jnp.int32, (8, 2048), 0)
    stat[...] = jnp.where(row == 0, top, jnp.where(row == 1, total, dots))
    stat_copy = remote(stat, strecv, sts, str_, sib, h)
    stat_copy.start()
    w_step(*STEPS_1)
    stat_copy.wait_recv()
    m_own, m_far = stat[0:1], strecv[0:1]
    m_all = jnp.maximum(m_own, m_far)
    f_own = jnp.exp2((m_own - m_all) * EXP_SCALE)
    f_far = jnp.exp2((m_far - m_all) * EXP_SCALE)
    l_all = stat[1:2] * f_own + strecv[1:2] * f_far
    d_all = (stat[2:3] * f_own + strecv[2:3] * f_far) / l_all
    stat_copy.wait_send()
    stat[0:1] = m_all
    stat[1:2] = 1.0 / l_all
    stat[2:3] = d_all

    def dk_copy(j):
        return remote(
            sendbuf.at[j], dkvrecv.at[j], dks.at[j], dkr.at[j], lax.rem(s - 2 * j + 32, 32), h
        )

    def backward(i, _):
        j = SPAN - 1 - i

        @pl.when(chip >= j)
        def _():
            for g in range(GROUP):
                cols = slice(g * 256, (g + 1) * 256)
                factor = jnp.exp2((mxb[j, 0:1, cols] - stat[0:1, cols]) * EXP_SCALE)
                factor = factor * stat[1:2, cols]
                probs = ebuf[j, :, cols] * factor
                pbuf[:, cols] = probs.astype(jnp.bfloat16)
                grad_l = probs * (dpbuf[j, :, cols] - stat[2:3, cols])
                dsbuf[j, :, cols] = grad_l.astype(jnp.bfloat16)
            grad_k = jnp.zeros((ROWS, HD), jnp.float32)
            grad_v = jnp.zeros((ROWS, HD), jnp.float32)
            for g in range(GROUP):
                cols, head = slice(g * 256, (g + 1) * 256), slice(g * HD, (g + 1) * HD)
                grad_k = grad_k + jnp.dot(
                    dsbuf[j, :, cols], qall[:, head], preferred_element_type=jnp.float32
                )
                grad_v = grad_v + jnp.dot(
                    pbuf[:, cols], goall[:, head], preferred_element_type=jnp.float32
                )
            grad_k = grad_k * SCALE
            ownbuf[:, :HD] = grad_k
            ownbuf[:, HD:] = grad_v

            @pl.when(j > 0)
            def _():
                sendbuf[j, :, :HD] = grad_k.astype(jnp.bfloat16)
                sendbuf[j, :, HD:] = grad_v.astype(jnp.bfloat16)
                dk_copy(j).start()

        return 0

    lax.fori_loop(0, SPAN, backward, 0)
    w_step(*STEPS_2)

    key_t = jnp.concatenate([jnp.transpose(kvbuf[j, :, :HD]) for j in range(SPAN)], axis=1)
    for g in range(GROUP):
        grad_t = jnp.dot(
            key_t,
            dsbuf[:, :, g * 256:(g + 1) * 256].reshape(SPAN * ROWS, 256),
            preferred_element_type=jnp.float32,
        )
        dqbuf[:, g * HD:(g + 1) * HD] = jnp.transpose(grad_t) * SCALE
    dq_copy = remote(dqbuf.at[pl.ds((1 - core) * ROWS, ROWS)], dqrecv, dqs, dqr, sib, h)
    dq_copy.start()
    w_step(*STEPS_3)

    acc = ownbuf[...]
    ownbuf[...] = acc
    for j in range(1, SPAN):

        @pl.when(chip + j <= 15)
        def _():
            dk_copy(j).wait_recv()
            ownbuf[...] += dkvrecv[j].astype(jnp.float32)

    grad_kv = ownbuf[...].astype(jnp.bfloat16)
    gbuf[h] = grad_kv
    out_kv = pltpu.make_async_copy(gbuf.at[h], gkv_ref, loc.at[7])
    out_kv.start()

    z_send = remote(gbuf.at[h], gbuf.at[h], g1s, g1r, s, x * 2 + 1 - zh)
    z_wait = remote(gbuf.at[h], gbuf.at[x * 2 + 1 - zh], g1s, g1r, s, x * 2 + 1 - zh)
    z_send.start()

    def gx_copy(k, far):
        hh = (x * 2 + 1 - zh) if far else h
        xt = lax.rem(x + k, 4)
        n = k + (4 if far else 0)
        return remote(gbuf.at[hh], gbuf.at[hh], gxs.at[n], gxr.at[n], s, xt * 2 + zh)

    def gx_wait(k, far):
        xf = lax.rem(x + 4 - k, 4)
        hh = xf * 2 + ((1 - zh) if far else zh)
        n = k + (4 if far else 0)
        return remote(gbuf.at[hh], gbuf.at[hh], gxs.at[n], gxr.at[n], s, h)

    for k in range(1, 4):
        gx_copy(k, False).start()
    w_step(*STEPS_4)
    dq_copy.wait_recv()
    gqbuf[...] = (dqbuf[own_rows, :] + dqrecv[...]).astype(jnp.bfloat16)
    out_q = pltpu.make_async_copy(gqbuf, gq_ref, loc.at[8])
    out_q.start()
    w_step(*STEPS_5)
    z_wait.wait_recv()
    for k in range(1, 4):
        gx_copy(k, True).start()

    own_delta.wait()
    for k in range(1, 4):
        del_wait(k).wait_recv()
    def project(n):
        out = None
        for b in range(2):
            left = dbuf[:, :, b * 1024:(b + 1) * 1024].reshape(512, 1024)
            right = wbuf[b, n].reshape(512, 1024)
            part = lax.dot_general(left, right, NT, preferred_element_type=jnp.float32)
            out = part if out is None else out + part
        pbig[n] = out

    w_near()

    def near(k, _):
        project(lax.rem(y + 3 + k, 4))
        return 0

    lax.fori_loop(0, 3, near, 0)
    w_step(*STEPS_6)
    w_far()
    project(lax.rem(y + 2, 4))
    for k in range(1, 4):
        gx_wait(k, False).wait_recv()
        gx_wait(k, True).wait_recv()

    lane = lax.broadcasted_iota(jnp.int32, (8, 128), 1)
    sub = lax.broadcasted_iota(jnp.int32, (8, 128), 0)
    tile = jnp.zeros((8, 128), jnp.float32)
    for hh in range(8):
        grads = gbuf[hh].astype(jnp.float32)
        off = (hh % 2) * 256
        for i in range(4):
            prod = pbig[hh // 2, i * 128:(i + 1) * 128, off:off + 256] * grads
            prod = jnp.sum(prod.reshape(16, 8, 256), axis=0)
            prod = jnp.sum(prod, axis=0, keepdims=True)
            for n in range(2):
                value = jnp.sum(prod[:, n * 128:(n + 1) * 128], axis=1, keepdims=True)
                hit = (sub == 2 * i + zh) & (lane == 2 * hh + n)
                tile = jnp.where(hit, value, tile)
    tile = tile * (1.0 / 64.0)

    ring4, ring8 = (2, 1, 3, 0), (4, 3, 5, 2, 6, 1, 7, 0)
    plane = [(dx, dy, dc) for dx in ring4 for dy in ring4 for dc in (1, 0)][:-1]
    plane.sort(key=lambda o: -(min(o[0], 4 - o[0]) + min(o[1], 4 - o[1])))

    me = x * 8 + y * 2 + core

    def plane_copy(dx, dy, dc, wait=False):
        n = dx * 8 + dy * 2 + dc
        slot = me
        if wait:
            slot = lax.rem(x + 4 - dx, 4) * 8 + lax.rem(y + 4 - dy, 4) * 2
            slot = slot + lax.rem(core + dc, 2)
        c_ = lax.rem(core + dc, 2)
        seq = (lax.rem(y + dy, 4) * 4 + zl) * 2 + c_
        head = lax.rem(x + dx, 4) * 2 + zh
        return remote(arsrc.at[0], ar1.at[slot], a1s.at[n], a1r.at[n], seq, head)

    def z_copy(dz, wait=False):
        slot = lax.rem(z + 8 - dz, 8) if wait else z
        seq, head = at_yz(y, lax.rem(z + dz, 8), core)
        return remote(arsrc.at[1], ar2.at[slot], a2s.at[dz], a2r.at[dz], seq, head)

    arsrc[0] = tile
    for offset in plane:
        plane_copy(*offset).start()
    for offset in reversed(plane):
        plane_copy(*offset, True).wait_recv()
    ar1[me] = tile
    tile = jnp.sum(ar1[...], axis=0)
    arsrc[1] = tile
    for dz in ring8[:-1]:
        z_copy(dz).start()
    for dz in reversed(ring8[:-1]):
        z_copy(dz, True).wait_recv()
    ar2[z] = tile
    tile = jnp.sum(ar2[...], axis=0)
    sc_ref[...] = tile

    out_kv.wait()
    out_q.wait()
    docq_send.wait_send()
    q_copy.wait_send()
    go_copy.wait_send()
    for j in range(1, SPAN):

        @pl.when(chip + j <= 15)
        def _():
            doc_copy(j).wait_send()
            kv_copy(j).wait_send()

        @pl.when(chip >= j)
        def _():
            dk_copy(j).wait_send()

    for k in range(1, 4):
        del_copy(k).wait_send()
        gx_copy(k, False).wait_send()
        gx_copy(k, True).wait_send()
    for build, args in sent:
        build(*args).wait_send()
    dq_copy.wait_send()
    z_send.wait_send()
    for offset in plane:
        plane_copy(*offset).wait_send()
    for dz in ring8[:-1]:
        z_copy(dz).wait_send()


def finish(gq_in, gkv_in, tile_in, slot_ref, gq_out, gkv_out, sc_out):
    gq_out[...] = gq_in[...]
    gkv_out[...] = gkv_in[...]
    tile = tile_in[...]
    sub = lax.broadcasted_iota(jnp.int32, (8, 128), 0)
    scores = jnp.zeros((8, 128), jnp.float32)
    for i in range(8):
        scores = jnp.where(sub == slot_ref[i], tile[i:i + 1], scores)
    sc_out[...] = scores[:, :16]


def on_device(queries, keyval, grad_out, doc_ids, deltas, node_weights, layer_slot):
    vmem = pl.BlockSpec(memory_space=pltpu.VMEM)
    hbm = pl.BlockSpec(memory_space=pl.ANY)
    bf, f32, i32 = jnp.bfloat16, jnp.float32, jnp.int32
    V, D = pltpu.VMEM, pltpu.SemaphoreType.DMA
    scratch = [
        V((256, 1024), bf),
        V((256, 1024), bf),
        V((SPAN, 128, 256), bf),
        V((SPAN, 1, 128), i32),
        V((2, 1, 128), i32),
        V((128, 256), f32),
        V((SPAN, 128, 2048), f32),
        V((SPAN, 128, 2048), f32),
        V((SPAN, 8, 2048), f32),
        V((SPAN, 8, 2048), f32),
        V((SPAN, 8, 2048), f32),
        V((8, 2048), f32),
        V((8, 2048), f32),
        V((128, 2048), bf),
        V((SPAN, 128, 2048), bf),
        V((SPAN, 128, 256), bf),
        V((SPAN, 128, 256), bf),
        V((128, 256), f32),
        V((256, 1024), f32),
        V((128, 1024), bf),
        V((128, 1024), f32),
        V((4, 128, 2048), bf),
        V((2, 4, 4, 2, 64, 1024), bf),
        V((4, 512, 512), f32),
        V((8, 128, 256), bf),
        V((2, 8, 128), f32),
        V((32, 8, 128), f32),
        V((8, 8, 128), f32),
    ]
    sems = [
        9, 9, 9, 9, 2, 2, None, None, 9, 9, None, None, 4, 4, 9,
        4, 4, 20, 20, 10, 10, 16, 16, 8, 8, 24, 5, None, None, 8, 8,
        32, 32, 8, 8,
    ]
    scratch += [D if n is None else D((n,)) for n in sems]
    grad_query, grad_keyval, tile = pl.pallas_call(
        kernel,
        out_shape=(
            jax.ShapeDtypeStruct((128, 1024), bf),
            jax.ShapeDtypeStruct((128, 256), bf),
            jax.ShapeDtypeStruct((8, 128), f32),
        ),
        in_specs=[hbm, hbm, hbm, hbm, hbm, hbm],
        out_specs=(hbm, hbm, vmem),
        scratch_shapes=scratch,
        compiler_params=pltpu.CompilerParams(
            has_side_effects=True, collective_id=0, vmem_limit_bytes=60 * 1024 * 1024
        ),
    )(
        queries,
        keyval,
        grad_out,
        doc_ids.reshape(1, 128),
        deltas.reshape(128, 8192),
        node_weights.T,
    )
    return pl.pallas_call(
        finish,
        out_shape=(
            jax.ShapeDtypeStruct((128, 1024), bf),
            jax.ShapeDtypeStruct((128, 256), bf),
            jax.ShapeDtypeStruct((8, 16), f32),
        ),
        in_specs=[vmem, vmem, vmem, pl.BlockSpec(memory_space=pltpu.SMEM)],
        out_specs=(vmem, vmem, vmem),
    )(grad_query, grad_keyval, tile, layer_slot)


def solution(mesh):
    return jax.shard_map(
        on_device,
        mesh=mesh,
        in_specs=(
            P("seq", "head"),
            P("seq", "head"),
            P("seq", "head"),
            P("seq"),
            P("head", "seq", None),
            P("head", "seq"),
            P(),
        ),
        out_specs=(P("seq", "head"), P("seq", "head"), P()),
        check_vma=False,
    )
```

```python
import math

import jax
import jax.numpy as jnp
from jax import lax
from jax.experimental import pallas as pl
from jax.experimental.pallas import tpu as pltpu
from jax.sharding import PartitionSpec as P

HD = 128
GROUP = 8
ROWS = 128
SPAN = 9
CUT = 16
FORWARD_STEPS = ((1, (0, 1)), (3, (2, 3)), (5, (4, 5)), (7, (6,)))
STEPS_1, STEPS_2, STEPS_3, STEPS_4, STEPS_5, STEPS_6 = (7, 8), (9,), (), (10, 11), (), (12,)
NEG = -1e30
FLOOR = -1e29
SCALE = 1.0 / math.sqrt(HD)
EXP_SCALE = SCALE * math.log2(math.e)
MESH = pl.DeviceIdType.MESH
NT = (((1,), (1,)), ((), ()))


def remote(src, dst, send, recv, seq, head):
    return pltpu.make_async_remote_copy(
        src_ref=src,
        dst_ref=dst,
        send_sem=send,
        recv_sem=recv,
        device_id=(seq, head),
        device_id_type=MESH,
    )


def kernel(
    q_ref,
    kv_ref,
    go_ref,
    doc_ref,
    del_ref,
    wt_ref,
    gq_ref,
    gkv_ref,
    sc_ref,
    qall,
    goall,
    kvbuf,
    docbuf,
    docq,
    bias,
    ebuf,
    dpbuf,
    mxb,
    lsb,
    dsb,
    stat,
    strecv,
    pbuf,
    dsbuf,
    sendbuf,
    dkvrecv,
    ownbuf,
    dqbuf,
    gqbuf,
    dqrecv,
    dbuf,
    wbuf,
    pbig,
    gbuf,
    arsrc,
    ar1,
    ar2,
    kvs,
    kvr,
    docs,
    docr,
    qs,
    qr,
    sts,
    str_,
    dks,
    dkr,
    dqs,
    dqr,
    dls,
    dlr,
    loc,
    ays,
    ayr,
    azs,
    azr,
    bzs,
    bzr,
    bys,
    byr,
    bos,
    bor,
    fs,
    fr,
    g1s,
    g1r,
    gxs,
    gxr,
    a1s,
    a1r,
    a2s,
    a2r,
):
    s = lax.axis_index("seq")
    h = lax.axis_index("head")
    core = lax.rem(s, 2)
    chip = s // 2
    zl = lax.rem(chip, 4)
    y = chip // 4
    zh = lax.rem(h, 2)
    x = h // 2
    z = zh * 4 + zl
    sib = s + 1 - 2 * core

    def at_yz(y_, z_, c_):
        return (y_ * 4 + lax.rem(z_, 4)) * 2 + c_, x * 2 + z_ // 4

    def kv_copy(j):
        return remote(kv_ref, kvbuf.at[j], kvs.at[j], kvr.at[j], lax.rem(s + 2 * j, 32), h)

    def doc_copy(j):
        return remote(doc_ref, docbuf.at[j], docs.at[j], docr.at[j], lax.rem(s + 2 * j, 32), h)

    own_rows = pl.ds(core * ROWS, ROWS)
    far_rows = pl.ds((1 - core) * ROWS, ROWS)
    q_copy = remote(q_ref, qall.at[own_rows], qs.at[0], qr.at[0], sib, h)
    q_wait = remote(q_ref, qall.at[far_rows], qs.at[0], qr.at[0], sib, h)
    go_copy = remote(go_ref, goall.at[own_rows], qs.at[1], qr.at[1], sib, h)
    go_wait = remote(go_ref, goall.at[far_rows], qs.at[1], qr.at[1], sib, h)
    own = [
        pltpu.make_async_copy(src, dst, loc.at[2 + n])
        for n, (src, dst) in enumerate(
            (
                (q_ref, qall.at[own_rows]),
                (go_ref, goall.at[own_rows]),
                (kv_ref, kvbuf.at[0]),
                (doc_ref, docbuf.at[0]),
                (doc_ref, docq.at[core]),
            )
        )
    ]
    for copy in own:
        copy.start()

    barrier = pltpu.get_barrier_semaphore()

    def greet(seq, head):
        pl.semaphore_signal(barrier, inc=1, device_id=(seq, head), device_id_type=MESH)

    for k in range(1, 16):
        greet(lax.rem(s + 2 * k, 32), h)
    for k in range(4):
        greet(lax.rem(y + k, 4) * 8 + zl * 2 + 1 - core, h)
        greet(y * 8 + k * 2 + core, x * 2 + 1 - zh)
    for k in range(1, 4):
        for n in range(4):
            for c_ in range(2):
                greet((n * 4 + zl) * 2 + c_, lax.rem(x + k, 4) * 2 + zh)
    pl.semaphore_wait(barrier, 47)

    LA, LB = pl.ds(0, CUT), pl.ds(CUT, 64 - CUT)
    sent = {}

    def send(build, *args):
        build(*args).start()
        sent[(build, args)] = True

    def piece(r, m, rows, c_=None):
        o = lax.rem(z + r, 8)
        return wbuf.at[
            o // 4, lax.rem(y + 4 - m, 4), lax.rem(o, 4), core if c_ is None else c_, rows
        ]

    def to_y(k):
        return at_yz(lax.rem(y + k, 4), z, core)

    def to_z(d):
        return at_yz(y, lax.rem(z + d + 8, 8), core)

    def ay(k, wait=False):
        dst = piece(0, k if wait else 0, LA)
        return remote(wt_ref.at[LA], dst, ays.at[k], ayr.at[k], *to_y(k))

    def az(d, k, half, wait=False):
        o = lax.rem(z + (-d * (k if wait else k - 1)) % 8, 8)
        ref = wbuf.at[o // 4, pl.ds(half * 2, 2), lax.rem(o, 4), core, LA]
        n = ((d < 0) * 5 + k) * 2 + half
        return remote(ref, ref, azs.at[n], azr.at[n], *to_z(d))

    def bz(d, k, wait=False):
        ref = piece((-d * (k if wait else k - 1)) % 8, 0, LB)
        src = wt_ref.at[LB] if k == 1 else ref
        n = (d < 0) * 5 + k
        return remote(src, ref, bzs.at[n], bzr.at[n], *to_z(d))

    def by(d, r, wait=False):
        ref = piece(r, (d % 4) if wait else 0, LB)
        src = wt_ref.at[LB] if r == 0 else ref
        n = (d < 0) * 8 + r
        return remote(src, ref, bys.at[n], byr.at[n], *to_y(d % 4))

    def bo(d, r, wait=False):
        ref = piece(r, 2 if wait else d % 4, LB)
        return remote(ref, ref, bos.at[r], bor.at[r], *to_y(d % 4))

    def fa(r):
        o = lax.rem(z + r, 8)
        ref = wbuf.at[o // 4, :, lax.rem(o, 4), core, LA]
        return remote(ref, ref, fs.at[r], fr.at[0], sib, h)

    def fb(m):
        ref = wbuf.at[:, lax.rem(y + 4 - m, 4), :, core, LB]
        return remote(ref, ref, fs.at[8 + m], fr.at[1 + m // 2 + m % 2], sib, h)

    def fb_one(r):
        ref = piece(r, 2, LB)
        return remote(ref, ref, fs.at[16 + r], fr.at[4], sib, h)

    own_w = pltpu.make_async_copy(wt_ref, wbuf.at[zh, y, zl, core], loc.at[1])
    own_w.start()
    for d in (1, -1):
        send(bz, d, 1)
    for k in (1, 3, 2):
        send(ay, k)
    for d in (1, -1):
        send(by, d, 0)
    STEPS = {1: 4, -1: 3}

    def a_ring(k):
        for half in range(2):
            for d in (1, -1):
                if k <= STEPS[d]:
                    az(d, k, half, True).wait_recv()
                    if k < STEPS[d]:
                        send(az, d, k + 1, half)
        for r in sorted({k, -k % 8}):
            send(fa, r)

    def b_ring(k):
        for d in (1, -1):
            if k <= STEPS[d]:
                bz(d, k, True).wait_recv()
                if k < STEPS[d]:
                    send(bz, d, k + 1)
                r = (-d * k) % 8
                send(by, 1, r)
                send(by, -1, r)
        if k == 4:
            send(fb, 0)

    def b_side(k):
        for r in sorted({k, -k % 8}):
            for d in (1, -1):
                by(d, r, True).wait_recv()
                if (d > 0) == (r < 4):
                    send(bo, d, r)
        if k == 4:
            send(fb, 1)
            send(fb, 3)

    def b_far(k):
        for r in sorted({k, -k % 8}):
            bo(1 if r < 4 else -1, r, True).wait_recv()
            send(fb_one, r)

    def a_side():
        own_w.wait()
        for k in (1, 3, 2):
            ay(k, True).wait_recv()
        for half in range(2):
            send(az, 1, 1, half)
            send(az, -1, 1, half)
        send(fa, 0)

    plan = (
        ((b_ring, 1), (a_side,)),
        ((b_side, 0),),
        ((b_ring, 2),),
        ((a_ring, 1),),
        ((b_side, 1), (b_far, 0)),
        ((b_ring, 3),),
        ((a_ring, 2),),
        ((b_side, 2), (b_far, 1)),
        ((b_ring, 4),),
        ((a_ring, 3),),
        ((b_side, 3), (b_far, 2)),
        ((a_ring, 4), (b_side, 4), (b_far, 3)),
        ((b_far, 4),),
    )

    def w_step(*ns):
        for n in ns:
            for job in plan[n]:
                job[0](*job[1:])

    def w_near():
        ref = wbuf.at[:, :, :, 1 - core, LA]
        remote(ref, ref, fs.at[0], fr.at[0], sib, h).wait_recv()
        for m in (0, 1, 3):
            ref = wbuf.at[:, lax.rem(y + 4 - m, 4), :, 1 - core, LB]
            remote(ref, ref, fs.at[0], fr.at[1 + m // 2 + m % 2], sib, h).wait_recv()

    def w_far():
        ref = wbuf.at[:, lax.rem(y + 2, 4), :, 1 - core, LB]
        remote(ref, ref, fs.at[0], fr.at[4], sib, h).wait_recv()

    docq_send = remote(doc_ref, docq.at[core], docs.at[0], docr.at[0], sib, h)
    docq_wait = remote(doc_ref, docq.at[1 - core], docs.at[0], docr.at[0], sib, h)
    docq_send.start()
    for j in range(1, SPAN):

        @pl.when(chip + j <= 15)
        def _():
            doc_copy(j).start()
            kv_copy(j).start()

    q_copy.start()
    go_copy.start()

    def del_copy(k):
        xt = lax.rem(x + k, 4)
        return remote(
            del_ref.at[:, pl.ds(xt * 2048, 2048)],
            dbuf.at[x],
            dls.at[k],
            dlr.at[k],
            s,
            xt * 2 + zh,
        )

    def del_wait(k):
        xf = lax.rem(x + 4 - k, 4)
        return remote(
            del_ref.at[:, pl.ds(xf * 2048, 2048)],
            dbuf.at[xf],
            dls.at[k],
            dlr.at[k],
            s,
            xf * 2 + zh,
        )

    for k in range(1, 4):
        del_copy(k).start()
    own_delta = pltpu.make_async_copy(
        del_ref.at[:, pl.ds(x * 2048, 2048)], dbuf.at[x], loc.at[0]
    )
    own_delta.start()

    for j in range(SPAN):

        @pl.when(chip < j)
        def _():
            mxb[j] = jnp.full((8, 2048), FLOOR, jnp.float32)
            lsb[j] = jnp.zeros((8, 2048), jnp.float32)
            dsb[j] = jnp.zeros((8, 2048), jnp.float32)
            kvbuf[j] = jnp.zeros((ROWS, 256), jnp.bfloat16)
            dsbuf[j] = jnp.zeros((ROWS, 2048), jnp.bfloat16)

    for copy in own:
        copy.wait()
    docq_wait.wait_recv()
    q_wait.wait_recv()
    go_wait.wait_recv()

    def forward(j, _):
        @pl.when(chip >= j)
        def _():
            @pl.when(j > 0)
            def _():
                doc_copy(j).wait_recv()
                kv_copy(j).wait_recv()

            ids = docbuf[j]
            drow = jnp.concatenate((docq[0], docq[1]), axis=1)
            low = jnp.zeros((1, 256), jnp.float32)
            for v in range(3):
                count = jnp.sum((ids == v).astype(jnp.float32), axis=1, keepdims=True)
                low = low + jnp.where(drow > v, count, 0.0)
            place = lax.broadcasted_iota(jnp.int32, (ROWS, 256), 0)
            token = lax.broadcasted_iota(jnp.int32, (ROWS, 256), 1)
            high = jnp.where(j == 0, token - core * ROWS, ROWS)
            keep = (place >= low.astype(jnp.int32)) & (place <= high)
            bias[...] = jnp.where(keep, 0.0, NEG)
            key_rows = kvbuf[j, :, :HD]
            value_rows = kvbuf[j, :, HD:]
            for g in range(GROUP):
                cols = slice(g * 256, (g + 1) * 256)
                logits = lax.dot_general(
                    key_rows, qall[:, g * HD:(g + 1) * HD], NT, preferred_element_type=jnp.float32
                )
                grad_p = lax.dot_general(
                    value_rows, goall[:, g * HD:(g + 1) * HD], NT, preferred_element_type=jnp.float32
                )
                logits = logits + bias[...]
                top = jnp.maximum(jnp.max(logits, axis=0, keepdims=True), FLOOR)
                weight = jnp.exp2((logits - top) * EXP_SCALE)
                ebuf[j, :, cols] = weight
                dpbuf[j, :, cols] = grad_p
                mxb[j, :, cols] = jnp.broadcast_to(top, (8, 256))
                lsb[j, :, cols] = jnp.sum(weight.reshape(16, 8, 256), axis=0)
                dsb[j, :, cols] = jnp.sum((weight * grad_p).reshape(16, 8, 256), axis=0)

        for n, ns in FORWARD_STEPS:

            @pl.when(j == n)
            def _():
                w_step(*ns)

        return 0

    lax.fori_loop(0, SPAN, forward, 0)

    top = mxb[0]
    for j in range(1, SPAN):
        top = jnp.maximum(top, mxb[j])
    total = jnp.zeros((8, 2048), jnp.float32)
    dots = jnp.zeros((8, 2048), jnp.float32)
    for j in range(SPAN):
        factor = jnp.exp2((mxb[j] - top) * EXP_SCALE)
        total = total + factor * lsb[j]
        dots = dots + factor * dsb[j]
    total = jnp.sum(total, axis=0, keepdims=True)
    dots = jnp.sum(dots, axis=0, keepdims=True)
    row = lax.broadcasted_iota(jnp.int32, (8, 2048), 0)
    stat[...] = jnp.where(row == 0, top, jnp.where(row == 1, total, dots))
    stat_copy = remote(stat, strecv, sts, str_, sib, h)
    stat_copy.start()
    w_step(*STEPS_1)
    stat_copy.wait_recv()
    m_own, m_far = stat[0:1], strecv[0:1]
    m_all = jnp.maximum(m_own, m_far)
    f_own = jnp.exp2((m_own - m_all) * EXP_SCALE)
    f_far = jnp.exp2((m_far - m_all) * EXP_SCALE)
    l_all = stat[1:2] * f_own + strecv[1:2] * f_far
    d_all = (stat[2:3] * f_own + strecv[2:3] * f_far) / l_all
    stat_copy.wait_send()
    stat[0:1] = m_all
    stat[1:2] = 1.0 / l_all
    stat[2:3] = d_all

    def dk_copy(j):
        return remote(
            sendbuf.at[j], dkvrecv.at[j], dks.at[j], dkr.at[j], lax.rem(s - 2 * j + 32, 32), h
        )

    def backward(i, _):
        j = SPAN - 1 - i

        @pl.when(chip >= j)
        def _():
            for g in range(GROUP):
                cols = slice(g * 256, (g + 1) * 256)
                factor = jnp.exp2((mxb[j, 0:1, cols] - stat[0:1, cols]) * EXP_SCALE)
                factor = factor * stat[1:2, cols]
                probs = ebuf[j, :, cols] * factor
                pbuf[:, cols] = probs.astype(jnp.bfloat16)
                grad_l = probs * (dpbuf[j, :, cols] - stat[2:3, cols])
                dsbuf[j, :, cols] = grad_l.astype(jnp.bfloat16)
            grad_k = jnp.zeros((ROWS, HD), jnp.float32)
            grad_v = jnp.zeros((ROWS, HD), jnp.float32)
            for g in range(GROUP):
                cols, head = slice(g * 256, (g + 1) * 256), slice(g * HD, (g + 1) * HD)
                grad_k = grad_k + jnp.dot(
                    dsbuf[j, :, cols], qall[:, head], preferred_element_type=jnp.float32
                )
                grad_v = grad_v + jnp.dot(
                    pbuf[:, cols], goall[:, head], preferred_element_type=jnp.float32
                )
            grad_k = grad_k * SCALE
            ownbuf[:, :HD] = grad_k
            ownbuf[:, HD:] = grad_v

            @pl.when(j > 0)
            def _():
                sendbuf[j, :, :HD] = grad_k.astype(jnp.bfloat16)
                sendbuf[j, :, HD:] = grad_v.astype(jnp.bfloat16)
                dk_copy(j).start()

        return 0

    lax.fori_loop(0, SPAN, backward, 0)
    w_step(*STEPS_2)

    key_t = jnp.concatenate([jnp.transpose(kvbuf[j, :, :HD]) for j in range(SPAN)], axis=1)
    for g in range(GROUP):
        grad_t = jnp.dot(
            key_t,
            dsbuf[:, :, g * 256:(g + 1) * 256].reshape(SPAN * ROWS, 256),
            preferred_element_type=jnp.float32,
        )
        dqbuf[:, g * HD:(g + 1) * HD] = jnp.transpose(grad_t) * SCALE
    dq_copy = remote(dqbuf.at[pl.ds((1 - core) * ROWS, ROWS)], dqrecv, dqs, dqr, sib, h)
    dq_copy.start()
    w_step(*STEPS_3)

    acc = ownbuf[...]
    ownbuf[...] = acc
    for j in range(1, SPAN):

        @pl.when(chip + j <= 15)
        def _():
            dk_copy(j).wait_recv()
            ownbuf[...] += dkvrecv[j].astype(jnp.float32)

    grad_kv = ownbuf[...].astype(jnp.bfloat16)
    gbuf[h] = grad_kv
    out_kv = pltpu.make_async_copy(gbuf.at[h], gkv_ref, loc.at[7])
    out_kv.start()

    z_send = remote(gbuf.at[h], gbuf.at[h], g1s, g1r, s, x * 2 + 1 - zh)
    z_wait = remote(gbuf.at[h], gbuf.at[x * 2 + 1 - zh], g1s, g1r, s, x * 2 + 1 - zh)
    z_send.start()

    def gx_copy(k, far):
        hh = (x * 2 + 1 - zh) if far else h
        xt = lax.rem(x + k, 4)
        n = k + (4 if far else 0)
        return remote(gbuf.at[hh], gbuf.at[hh], gxs.at[n], gxr.at[n], s, xt * 2 + zh)

    def gx_wait(k, far):
        xf = lax.rem(x + 4 - k, 4)
        hh = xf * 2 + ((1 - zh) if far else zh)
        n = k + (4 if far else 0)
        return remote(gbuf.at[hh], gbuf.at[hh], gxs.at[n], gxr.at[n], s, h)

    for k in range(1, 4):
        gx_copy(k, False).start()
    w_step(*STEPS_4)
    dq_copy.wait_recv()
    gqbuf[...] = (dqbuf[own_rows, :] + dqrecv[...]).astype(jnp.bfloat16)
    out_q = pltpu.make_async_copy(gqbuf, gq_ref, loc.at[8])
    out_q.start()
    w_step(*STEPS_5)
    z_wait.wait_recv()
    for k in range(1, 4):
        gx_copy(k, True).start()

    own_delta.wait()
    for k in range(1, 4):
        del_wait(k).wait_recv()
    def project(n):
        out = None
        for b in range(2):
            left = dbuf[:, :, b * 1024:(b + 1) * 1024].reshape(512, 1024)
            right = wbuf[b, n].reshape(512, 1024)
            part = lax.dot_general(left, right, NT, preferred_element_type=jnp.float32)
            out = part if out is None else out + part
        pbig[n] = out

    w_near()

    def near(k, _):
        project(lax.rem(y + 3 + k, 4))
        return 0

    lax.fori_loop(0, 3, near, 0)
    w_step(*STEPS_6)
    w_far()
    project(lax.rem(y + 2, 4))
    for k in range(1, 4):
        gx_wait(k, False).wait_recv()
        gx_wait(k, True).wait_recv()

    lane = lax.broadcasted_iota(jnp.int32, (8, 128), 1)
    sub = lax.broadcasted_iota(jnp.int32, (8, 128), 0)
    tile = jnp.zeros((8, 128), jnp.float32)
    for hh in range(8):
        grads = gbuf[hh].astype(jnp.float32)
        off = (hh % 2) * 256
        for i in range(4):
            prod = pbig[hh // 2, i * 128:(i + 1) * 128, off:off + 256] * grads
            prod = jnp.sum(prod.reshape(16, 8, 256), axis=0)
            prod = jnp.sum(prod, axis=0, keepdims=True)
            for n in range(2):
                value = jnp.sum(prod[:, n * 128:(n + 1) * 128], axis=1, keepdims=True)
                hit = (sub == 2 * i + zh) & (lane == 2 * hh + n)
                tile = jnp.where(hit, value, tile)
    tile = tile * (1.0 / 64.0)

    ring4, ring8 = (2, 1, 3, 0), (4, 3, 5, 2, 6, 1, 7, 0)
    plane = [(dx, dy, dc) for dx in ring4 for dy in ring4 for dc in (1, 0)][:-1]
    plane.sort(key=lambda o: -(min(o[0], 4 - o[0]) + min(o[1], 4 - o[1])))

    me = x * 8 + y * 2 + core

    def plane_copy(dx, dy, dc, wait=False):
        n = dx * 8 + dy * 2 + dc
        slot = me
        if wait:
            slot = lax.rem(x + 4 - dx, 4) * 8 + lax.rem(y + 4 - dy, 4) * 2
            slot = slot + lax.rem(core + dc, 2)
        c_ = lax.rem(core + dc, 2)
        seq = (lax.rem(y + dy, 4) * 4 + zl) * 2 + c_
        head = lax.rem(x + dx, 4) * 2 + zh
        return remote(arsrc.at[0], ar1.at[slot], a1s.at[n], a1r.at[n], seq, head)

    def z_copy(dz, wait=False):
        slot = lax.rem(z + 8 - dz, 8) if wait else z
        seq, head = at_yz(y, lax.rem(z + dz, 8), core)
        return remote(arsrc.at[1], ar2.at[slot], a2s.at[dz], a2r.at[dz], seq, head)

    arsrc[0] = tile
    for offset in plane:
        plane_copy(*offset).start()

    out_kv.wait()
    out_q.wait()
    docq_send.wait_send()
    q_copy.wait_send()
    go_copy.wait_send()
    for j in range(1, SPAN):

        @pl.when(chip + j <= 15)
        def _():
            doc_copy(j).wait_send()
            kv_copy(j).wait_send()

        @pl.when(chip >= j)
        def _():
            dk_copy(j).wait_send()

    for k in range(1, 4):
        del_copy(k).wait_send()
        gx_copy(k, False).wait_send()
        gx_copy(k, True).wait_send()
    for build, args in sent:
        build(*args).wait_send()
    dq_copy.wait_send()
    z_send.wait_send()

    for offset in reversed(plane):
        plane_copy(*offset, True).wait_recv()
    ar1[me] = tile
    tile = jnp.sum(ar1[...], axis=0)
    arsrc[1] = tile
    for dz in ring8[:-1]:
        z_copy(dz).start()
    for dz in reversed(ring8[:-1]):
        z_copy(dz, True).wait_recv()
    ar2[z] = tile
    tile = jnp.sum(ar2[...], axis=0)
    sc_ref[...] = tile

    for offset in plane:
        plane_copy(*offset).wait_send()
    for dz in ring8[:-1]:
        z_copy(dz).wait_send()


def finish(gq_in, gkv_in, tile_in, slot_ref, gq_out, gkv_out, sc_out):
    gq_out[...] = gq_in[...]
    gkv_out[...] = gkv_in[...]
    tile = tile_in[...]
    sub = lax.broadcasted_iota(jnp.int32, (8, 128), 0)
    scores = jnp.zeros((8, 128), jnp.float32)
    for i in range(8):
        scores = jnp.where(sub == slot_ref[i], tile[i:i + 1], scores)
    sc_out[...] = scores[:, :16]


def on_device(queries, keyval, grad_out, doc_ids, deltas, node_weights, layer_slot):
    vmem = pl.BlockSpec(memory_space=pltpu.VMEM)
    hbm = pl.BlockSpec(memory_space=pl.ANY)
    bf, f32, i32 = jnp.bfloat16, jnp.float32, jnp.int32
    V, D = pltpu.VMEM, pltpu.SemaphoreType.DMA
    scratch = [
        V((256, 1024), bf),
        V((256, 1024), bf),
        V((SPAN, 128, 256), bf),
        V((SPAN, 1, 128), i32),
        V((2, 1, 128), i32),
        V((128, 256), f32),
        V((SPAN, 128, 2048), f32),
        V((SPAN, 128, 2048), f32),
        V((SPAN, 8, 2048), f32),
        V((SPAN, 8, 2048), f32),
        V((SPAN, 8, 2048), f32),
        V((8, 2048), f32),
        V((8, 2048), f32),
        V((128, 2048), bf),
        V((SPAN, 128, 2048), bf),
        V((SPAN, 128, 256), bf),
        V((SPAN, 128, 256), bf),
        V((128, 256), f32),
        V((256, 1024), f32),
        V((128, 1024), bf),
        V((128, 1024), f32),
        V((4, 128, 2048), bf),
        V((2, 4, 4, 2, 64, 1024), bf),
        V((4, 512, 512), f32),
        V((8, 128, 256), bf),
        V((2, 8, 128), f32),
        V((32, 8, 128), f32),
        V((8, 8, 128), f32),
    ]
    sems = [
        9, 9, 9, 9, 2, 2, None, None, 9, 9, None, None, 4, 4, 9,
        4, 4, 20, 20, 10, 10, 16, 16, 8, 8, 24, 5, None, None, 8, 8,
        32, 32, 8, 8,
    ]
    scratch += [D if n is None else D((n,)) for n in sems]
    grad_query, grad_keyval, tile = pl.pallas_call(
        kernel,
        out_shape=(
            jax.ShapeDtypeStruct((128, 1024), bf),
            jax.ShapeDtypeStruct((128, 256), bf),
            jax.ShapeDtypeStruct((8, 128), f32),
        ),
        in_specs=[hbm, hbm, hbm, hbm, hbm, hbm],
        out_specs=(hbm, hbm, vmem),
        scratch_shapes=scratch,
        compiler_params=pltpu.CompilerParams(
            has_side_effects=True, collective_id=0, vmem_limit_bytes=60 * 1024 * 1024
        ),
    )(
        queries,
        keyval,
        grad_out,
        doc_ids.reshape(1, 128),
        deltas.reshape(128, 8192),
        node_weights.T,
    )
    return pl.pallas_call(
        finish,
        out_shape=(
            jax.ShapeDtypeStruct((128, 1024), bf),
            jax.ShapeDtypeStruct((128, 256), bf),
            jax.ShapeDtypeStruct((8, 16), f32),
        ),
        in_specs=[vmem, vmem, vmem, pl.BlockSpec(memory_space=pltpu.SMEM)],
        out_specs=(vmem, vmem, vmem),
    )(grad_query, grad_keyval, tile, layer_slot)


def solution(mesh):
    return jax.shard_map(
        on_device,
        mesh=mesh,
        in_specs=(
            P("seq", "head"),
            P("seq", "head"),
            P("seq", "head"),
            P("seq"),
            P("head", "seq", None),
            P("head", "seq"),
            P(),
        ),
        out_specs=(P("seq", "head"), P("seq", "head"), P()),
        check_vma=False,
    )
```
